128 devices in a mesh: param: 4 (over z_lo, core), space: 32 (over y, z_hi, x).
Axes of the slice: x: 4, y: 4, z: 4 (z_hi: 2, z_lo: 2; z = z_hi * 2 + z_lo), core: 2. Of those that a mesh axis runs over, the one named last changes fastest.
Arguments:
- fine_state: bfloat16 [64, 16, 64, 512], P('space', None, None, 'param'), may hold values from -6 to 6
- fine_tangent: bfloat16 [64, 16, 64, 512], P('space', None, None, 'param'), may hold values from -6 to 6
- down_weight: float32 [8, 512, 1024], P(None, 'space', 'param'), may hold values from -0.09375 to 0.09375
- conv_weight: float32 [27, 1024, 1024], P(None, 'space', 'param'), may hold values from -0.0390625 to 0.0390625
- up_weight: float32 [8, 1024, 512], P(None, 'space', 'param'), may hold values from -0.1875 to 0.1875
Outputs:
- state_out: bfloat16 [64, 16, 64, 512], P('space', None, None, 'param')
- tangent_out: bfloat16 [64, 16, 64, 512], P('space', None, None, 'param')
The draws below stay inside these ranges and needn't reach their ends.
All inputs are finite; a program needn't handle non-finite values.
Results may differ from the reference program's by a relative error of at most 0.0075.
Values may be sent and summed in bfloat16 or wider, within the bound.
A program may use at most 128 MiB of HBM per device.

```python
import jax
import jax.numpy as jnp

CF = 512
CC = 1024
CY = 8
CX = 32
CZ = 32
FZ = 64
FY = 16
FX = 64


def block_scale(key, extent, shards, least, high):
    gain = 1.0
    for axis_at, shards_of in shards:
        heights = jax.random.uniform(jax.random.fold_in(jax.random.fold_in(key, 6), axis_at), (shards_of,), jnp.float32, least / len(shards), high / len(shards))
        gain = gain * jnp.repeat(jnp.exp(heights), extent[axis_at] // shards_of).reshape((-1,) + (1,) * (len(extent) - 1 - axis_at))
    return gain


def noise(key, shape, spread, reach, shards=(), dtype=jnp.bfloat16):
    array = spread * jax.random.normal(key, shape, jnp.float32)
    if shards:
        array = array * block_scale(key, shape, shards, -0.22, 0.18)
    return jnp.clip(array, -reach, reach).astype(dtype)


def setup_inputs(seed: int = 0) -> dict:
    arg_keys = jax.random.split(jax.random.key(seed), 6)
    return {
        "fine_state": noise(arg_keys[0], (FZ, FY, FX, CF), 1.0, 6.0, ((0, 32), (3, 4))),
        "fine_tangent": noise(arg_keys[1], (FZ, FY, FX, CF), 1.0, 6.0, ((0, 32), (3, 4))),
        "down_weight": noise(arg_keys[2], (8, CF, CC), (8 * CF) ** -0.5, 0.09375, ((1, 32), (2, 4)), jnp.float32),
        "conv_weight": noise(arg_keys[3], (27, CC, CC), (27 * CC) ** -0.5, 0.0390625, ((1, 32), (2, 4)), jnp.float32),
        "up_weight": noise(arg_keys[4], (8, CC, CF), CC ** -0.5, 0.1875, ((1, 32), (2, 4)), jnp.float32),
    }


def silu_pair(primal, tangent):
    sigma = jax.nn.sigmoid(primal)
    return primal * sigma, sigma * (1.0 + primal * (1.0 - sigma)) * tangent


def strided_down(field, kernel):
    patches = field.reshape(CZ, 2, CY, 2, CX, 2, CF).transpose(0, 2, 4, 1, 3, 5, 6).reshape(CZ * CY * CX, 8 * CF)
    return jnp.dot(patches, kernel.reshape(8 * CF, CC), preferred_element_type=jnp.float32)


def cube_conv(field, kernel):
    padded = jnp.pad(field.reshape(CZ, CY, CX, CC), ((1, 1), (1, 1), (1, 1), (0, 0)))
    result = jnp.zeros((CZ * CY * CX, CC), jnp.float32)
    for tap_z in range(3):
        for tap_y in range(3):
            for tap_x in range(3):
                window = padded[tap_z:tap_z + CZ, tap_y:tap_y + CY, tap_x:tap_x + CX, :].reshape(CZ * CY * CX, CC)
                result = result + jnp.dot(window, kernel[9 * tap_z + 3 * tap_y + tap_x], preferred_element_type=jnp.float32)
    return result


def strided_up(field, kernel):
    product = jnp.dot(field, kernel.transpose(1, 0, 2).reshape(CC, 8 * CF), preferred_element_type=jnp.float32)
    return product.reshape(CZ, CY, CX, 2, 2, 2, CF).transpose(0, 3, 1, 4, 2, 5, 6).reshape(2 * CZ, 2 * CY, 2 * CX, CF)


def reference(fine_state, fine_tangent, down_weight, conv_weight, up_weight):
    down_kernel = down_weight.astype(jnp.bfloat16)
    cube_kernel = conv_weight.astype(jnp.bfloat16)
    up_kernel = up_weight.astype(jnp.bfloat16)
    first_pre = strided_down(fine_state, down_kernel)
    first_tan = strided_down(fine_tangent, down_kernel)
    first_val, first_dir = silu_pair(first_pre, first_tan)
    first_val = first_val.astype(jnp.bfloat16)
    first_dir = first_dir.astype(jnp.bfloat16)
    second_pre = cube_conv(first_val, cube_kernel)
    second_tan = cube_conv(first_dir, cube_kernel)
    second_val, second_dir = silu_pair(second_pre, second_tan)
    second_val = (second_val + first_val.astype(jnp.float32)).astype(jnp.bfloat16)
    second_dir = (second_dir + first_dir.astype(jnp.float32)).astype(jnp.bfloat16)
    state_out = strided_up(second_val, up_kernel).astype(jnp.bfloat16)
    tangent_out = strided_up(second_dir, up_kernel).astype(jnp.bfloat16)
    return (state_out, tangent_out)
```

```python
import jax
import jax.numpy as jnp
from jax import lax
from jax.experimental import pallas as pl
from jax.experimental.pallas import tpu as pltpu
from jax.sharding import PartitionSpec as P

MESH = pl.DeviceIdType.MESH
F32 = jnp.float32
BF16 = jnp.bfloat16


def silu_pair(primal, tangent):
    sigma = jax.nn.sigmoid(primal)
    return primal * sigma, sigma * (1.0 + primal * (1.0 - sigma)) * tangent


class Links:
    def __init__(self, send_sems, recv_sems, count):
        self.send_sems, self.recv_sems, self.count = send_sems, recv_sems, count
        self.used = 0
        self.sent = []

    def copy(self, src, dst, device, slot=None):
        at = self.used
        self.used += 1
        assert self.used <= self.count
        desc = pltpu.make_async_remote_copy(
            src_ref=src,
            dst_ref=dst,
            send_sem=self.send_sems.at[at],
            recv_sem=self.recv_sems.at[at] if slot is None else slot,
            device_id=device,
            device_id_type=MESH,
        )
        return desc

    def start(self, src, dst, device):
        desc = self.copy(src, dst, device)
        desc.start()
        self.sent.append((None, desc))
        return desc

    def drain(self):
        for cond, desc in self.sent:
            if cond is None:
                desc.wait_send()
            else:
                pl.when(cond)(desc.wait_send)


class Gather:
    def __init__(self, links, ref, at, devs, over_y):
        self.links, self.ref, self.devs, self.over_y = links, ref, devs, over_y
        self.y, self.zh, self.x = at
        self.xs = [self.x, (self.x + 3) % 4, (self.x + 1) % 4, (self.x + 2) % 4]
        self.first = {}
        self.second = {}

    def view(self, zh, x, y=None):
        if not self.over_y:
            return self.ref.at[zh, x]
        return self.ref.at[self.y if y is None else y, zh, x]

    def pair(self, x, y):
        return self.ref.at[y, :, x]

    def send(self, view, to):
        return self.links.start(view, view, self.devs[to])

    def start(self):
        own = self.view(self.zh, self.x)
        self.z = self.send(own, "zh")
        self.a_right = self.send(own, "right")
        self.a_left = self.send(own, "left")

    def after_z(self):
        self.z.wait_recv()
        other = self.view(1 - self.zh, self.x)
        self.b_right = self.send(other, "right")
        self.b_left = self.send(other, "left")

    def forward_x(self):
        self.a_right.wait_recv()
        self.f_right = self.send(self.view(self.zh, self.xs[1]), "right")
        self.b_left.wait_recv()
        self.f_left = self.send(self.view(1 - self.zh, self.xs[2]), "left")

    def wait_x1(self):
        self.b_right.wait_recv()
        self.a_left.wait_recv()

    def wait_x2(self):
        self.f_right.wait_recv()
        self.f_left.wait_recv()

    def start_y(self, g):
        block = self.pair(self.xs[g], self.y)
        self.first[g] = (self.send(block, "up"), self.send(block, "down"))

    def forward_y(self, g):
        up, down = self.first[g]
        up.wait_recv()
        a = self.send(self.ref.at[(self.y + 3) % 4, 0, self.xs[g]], "up")
        down.wait_recv()
        b = self.send(self.ref.at[(self.y + 1) % 4, 1, self.xs[g]], "down")
        self.second[g] = (a, b)

    def wait_y(self, g):
        for desc in self.second[g]:
            desc.wait_recv()


LINKS = 96


def kernel(
    fs, ft, wd32, wc32, wu32, out_s, out_t,
    ff, taps, wd_own, wd, wc, wu, part, part_in, first, first_z, apad, acc, sums, sums_in,
    top, up_acc, spread, send_sems, recv_sems, plane_sems, sum_sems, local_sem,
):
    p = lax.axis_index("param")
    s = lax.axis_index("space")
    zl, c = p // 2, p % 2
    y, zh, x = s // 8, (s // 4) % 2, s % 4

    def space(yy, zz, xx):
        return 8 * yy + 4 * zz + xx

    sib = (2 * zl + 1 - c, s)
    across = (2 * (1 - zl) + c, s)
    swap = (2 * (1 - zl) + c, space((y + 2) % 4, zh, x))
    devs = {
        "zh": (p, space(y, 1 - zh, x)),
        "right": (p, space(y, zh, (x + 1) % 4)),
        "left": (p, space(y, zh, (x + 3) % 4)),
        "up": (p, space((y + 1) % 4, zh, x)),
        "down": (p, space((y + 3) % 4, zh, x)),
    }
    partners = [sib, across, swap] + list(devs.values())
    barrier = pltpu.get_barrier_semaphore()
    for device in partners:
        pl.semaphore_signal(barrier, inc=1, device_id=device, device_id_type=MESH)

    placed = (y // 2) == zl
    wd_own[...] = wd32[...].astype(BF16)

    @pl.when(placed)
    def _():
        wd[y, zh, x] = wd_own[...]

    pl.semaphore_wait(barrier, len(partners))
    links = Links(send_sems, recv_sems, LINKS)

    moved = links.copy(wd_own, wd.at[(y + 2) % 4, zh, x], swap)
    links.sent.append((jnp.logical_not(placed), moved))
    pl.when(jnp.logical_not(placed))(moved.start)

    for f, fine in enumerate((fs, ft)):
        ff[...] = fine[...].astype(F32)
        for dz in range(2):
            for dy in range(2):
                for dx in range(2):
                    rows = ff[dz, :, dy, pl.ds(dx, 32, stride=2), :]
                    taps[c, 4 * dz + 2 * dy + dx, f] = rows.reshape(256, 128).astype(BF16)

    pl.when(jnp.logical_not(placed))(moved.wait_recv)
    at = (y, zh, x)
    gd = Gather(links, wd, at, devs, True)
    gc = Gather(links, wc, at, devs, False)
    gu = Gather(links, wu, at, devs, True)
    gd.start()
    fine_copy = links.start(taps.at[c], taps.at[c], sib)
    wc[zh, x] = wc32[...].astype(BF16)
    for t in range(4):
        for dx in range(2):
            wu[y, zh, x, t, :, 128 * dx : 128 * dx + 128] = wu32[2 * t + dx].astype(BF16)
    gd.after_z()
    gd.start_y(0)
    gd.forward_x()
    gd.wait_x1()
    gd.start_y(1)
    gd.start_y(2)
    gd.wait_x2()
    gd.start_y(3)
    gc.start()
    gd.forward_y(0)
    gd.forward_y(1)
    gd.forward_y(2)
    gc.after_z()
    gu.start()
    gd.forward_y(3)
    gu.after_z()
    fine_copy.wait_recv()
    for g in range(4):
        gd.wait_y(g)

    def down(half):
        total = None
        for t in range(8):
            rows = jnp.concatenate([taps[0, t], taps[1, t]], axis=-1).reshape(512, 256)
            weights = wd[pl.ds(2 * half, 2), :, :, t].reshape(256, 256)
            term = jnp.dot(rows, weights, preferred_element_type=F32)
            total = term if total is None else total + term
        return total

    part[...] = down(1 - zl).astype(BF16)
    part_copy = links.start(part, part_in, across)
    gc.forward_x()
    gu.forward_x()
    acc[0] = down(zl)
    gu.start_y(0)
    gu.wait_x1()
    gu.start_y(1)
    gu.start_y(2)
    part_copy.wait_recv()
    val, dir_ = silu_pair(
        acc[0, :256] + part_in[:256].astype(F32), acc[0, 256:] + part_in[256:].astype(F32)
    )
    first[0] = val.astype(BF16).reshape(8, 32, 256)
    first[1] = dir_.astype(BF16).reshape(8, 32, 256)
    first_copy = links.start(first, first_z, across)

    apad[:, :, pl.ds(0, 1)] = jnp.zeros((2, 6, 1, 32, 256), BF16)
    apad[:, :, pl.ds(9, 1)] = jnp.zeros((2, 6, 1, 32, 256), BF16)
    last_group = jnp.logical_and(x == 3, zh == 1)
    first_group = jnp.logical_and(x == 0, zh == 0)

    @pl.when(first_group)
    def _():
        apad[:, 0, pl.ds(1, 8)] = jnp.zeros((2, 8, 32, 256), BF16)

    @pl.when(last_group)
    def _():
        apad[:, 5, pl.ds(1, 8)] = jnp.zeros((2, 8, 32, 256), BF16)

    def window(slot):
        return apad.at[:, slot, pl.ds(1, 8)]

    def spread_planes(block, chunk):
        here = jnp.logical_and(chunk == y, x == y)
        main = links.copy(block, window(x + 1), (p, space(chunk, zh, y)), plane_sems.at[x + 1])
        away = jnp.logical_not(here)
        links.sent.append((away, main))
        pl.when(away)(main.start)

        @pl.when(here)
        def _():
            same = pltpu.make_async_copy(block, window(x + 1), local_sem)
            same.start()
            same.wait()

        after = jnp.logical_and(x == 3, s != 31)
        group = (s + 1) // 4
        high = links.copy(
            block, window(0), (p, space(chunk, group % 2, (group // 2) % 4)), plane_sems.at[0]
        )
        links.sent.append((after, high))
        pl.when(after)(high.start)
        before = jnp.logical_and(x == 0, s != 0)
        group = (s + 31) // 4
        low = links.copy(
            block, window(5), (p, space(chunk, group % 2, (group // 2) % 4)), plane_sems.at[5]
        )
        links.sent.append((before, low))
        pl.when(before)(low.start)

    spread_planes(first, p)
    gu.wait_x2()
    gu.start_y(3)
    first_copy.wait_recv()
    spread_planes(first_z, 2 * (1 - zl) + c)
    gc.wait_x1()
    gc.wait_x2()

    gets = c == y % 2
    for slot in range(6):
        hop = links.copy(window(slot), window(slot), sib, plane_sems.at[slot])
        arrives = None
        if slot == 0:
            arrives = jnp.logical_not(first_group)
        elif slot == 5:
            arrives = jnp.logical_not(last_group)
        else:
            inside = jnp.logical_and(x == slot - 1, y == slot - 1)
            arrives = jnp.logical_not(jnp.logical_and(gets, inside))
        pl.when(arrives)(hop.wait_recv)
        sends = gets
        if slot == 0:
            sends = jnp.logical_and(gets, jnp.logical_not(first_group))
        if slot == 5:
            sends = jnp.logical_and(gets, jnp.logical_not(last_group))
        links.sent.append((sends, hop))
        pl.when(sends)(hop.start)

    for g in range(4):
        gu.forward_y(g)

    edge = lax.broadcasted_iota(jnp.int32, (1, 32, 1), 1)

    for plane in range(4):
        for kz in range(3):
            for ky in range(3):
                rows = apad[:, plane + kz, ky : ky + 8].reshape(512, 256)
                for kx in range(3):
                    weights = wc[:, :, 9 * kz + 3 * ky + kx].reshape(256, 256)
                    term = jnp.dot(rows, weights, preferred_element_type=F32)
                    if kz == 0 and ky == 0:
                        acc[kx] = term
                    else:
                        acc[kx] += term
        low = pltpu.roll(acc[0], 1, 0).reshape(16, 32, 256)
        high = pltpu.roll(acc[2], 511, 0).reshape(16, 32, 256)
        total = acc[1].reshape(16, 32, 256)
        total = total + jnp.where(edge == 0, 0.0, low) + jnp.where(edge == 31, 0.0, high)
        sums[plane] = total.reshape(512, 256).astype(BF16)
        mine = jnp.logical_and(y == x, x == plane)
        away = jnp.logical_not(mine)
        part_sum = links.copy(
            sums.at[plane], sums_in.at[y], (p, space(x, zh, plane)), sum_sems.at[y]
        )
        links.sent.append((away, part_sum))
        pl.when(away)(part_sum.start)

        @pl.when(mine)
        def _():
            same = pltpu.make_async_copy(sums.at[plane], sums_in.at[y], local_sem)
            same.start()
            same.wait()

    for g in range(4):
        gu.wait_y(g)
    for k in range(4):
        mine = jnp.logical_and(y == x, y == k)
        desc = pltpu.make_async_remote_copy(
            src_ref=sums.at[0], dst_ref=sums_in.at[k], send_sem=send_sems.at[0],
            recv_sem=sum_sems.at[k], device_id=sib, device_id_type=MESH,
        )
        pl.when(jnp.logical_not(mine))(desc.wait_recv)

    total = sums_in[0].astype(F32) + sums_in[1].astype(F32)
    total = total + (sums_in[2].astype(F32) + sums_in[3].astype(F32))
    val, dir_ = silu_pair(total[:256], total[256:])
    top[p, :256] = (val + first[0].reshape(256, 256).astype(F32)).astype(BF16)
    top[p, 256:] = (dir_ + first[1].reshape(256, 256).astype(F32)).astype(BF16)
    cross = links.start(top.at[p], top.at[p], across)
    near = links.start(top.at[p], top.at[p], sib)

    def add_up(chunk, fresh):
        rows = top[chunk]
        for t in range(4):
            weights = wu[chunk, :, :, t].reshape(256, 256)
            term = jnp.dot(rows, weights, preferred_element_type=F32)
            if fresh:
                up_acc[t] = term
            else:
                up_acc[t] += term

    add_up(p, True)
    near.wait_recv()
    add_up(sib[0], False)
    cross.wait_recv()
    relay = links.start(top.at[across[0]], top.at[across[0]], sib)
    add_up(across[0], False)
    relay.wait_recv()
    add_up(2 * (1 - zl) + 1 - c, False)
    for f, out in enumerate((out_s, out_t)):
        for t in range(4):
            for dx in range(2):
                block = up_acc[t, 256 * f : 256 * f + 256, 128 * dx : 128 * dx + 128]
                spread[t // 2, :, t % 2, pl.ds(dx, 32, stride=2), :] = block.reshape(8, 32, 128)
        out[...] = spread[...].astype(BF16)
    links.drain()


def local(fine_state, fine_tangent, down_weight, conv_weight, up_weight):
    vmem = pl.BlockSpec(memory_space=pltpu.VMEM)
    fine = (2, 8, 2, 64, 128)
    shape = jax.ShapeDtypeStruct(fine, BF16)
    state, tangent = pl.pallas_call(
        kernel,
        out_shape=(shape, shape),
        in_specs=[vmem] * 5,
        out_specs=(vmem, vmem),
        scratch_shapes=[
            pltpu.VMEM(fine, F32),
            pltpu.VMEM((2, 8, 2, 256, 128), BF16),
            pltpu.VMEM((8, 16, 256), BF16),
            pltpu.VMEM((4, 2, 4, 8, 16, 256), BF16),
            pltpu.VMEM((2, 4, 27, 32, 256), BF16),
            pltpu.VMEM((4, 2, 4, 4, 32, 256), BF16),
            pltpu.VMEM((512, 256), BF16),
            pltpu.VMEM((512, 256), BF16),
            pltpu.VMEM((2, 8, 32, 256), BF16),
            pltpu.VMEM((2, 8, 32, 256), BF16),
            pltpu.VMEM((2, 6, 10, 32, 256), BF16),
            pltpu.VMEM((3, 512, 256), F32),
            pltpu.VMEM((4, 512, 256), BF16),
            pltpu.VMEM((4, 512, 256), BF16),
            pltpu.VMEM((4, 512, 256), BF16),
            pltpu.VMEM((4, 512, 256), F32),
            pltpu.VMEM(fine, F32),
            pltpu.SemaphoreType.DMA((LINKS,)),
            pltpu.SemaphoreType.DMA((LINKS,)),
            pltpu.SemaphoreType.DMA((6,)),
            pltpu.SemaphoreType.DMA((4,)),
            pltpu.SemaphoreType.DMA,
        ],
        compiler_params=pltpu.CompilerParams(
            collective_id=0, has_side_effects=True, vmem_limit_bytes=56 * 2**20
        ),
    )(fine_state.reshape(fine), fine_tangent.reshape(fine), down_weight, conv_weight, up_weight)
    return state.reshape(fine_state.shape), tangent.reshape(fine_state.shape)


def solution(mesh):
    in_specs = (
        P("space", None, None, "param"),
        P("space", None, None, "param"),
        P(None, "space", "param"),
        P(None, "space", "param"),
        P(None, "space", "param"),
    )
    out_specs = (P("space", None, None, "param"), P("space", None, None, "param"))
    return jax.shard_map(local, mesh=mesh, in_specs=in_specs, out_specs=out_specs, check_vma=False)
```

```python
import jax
import jax.numpy as jnp
from jax import lax
from jax.experimental import pallas as pl
from jax.experimental.pallas import tpu as pltpu
from jax.sharding import PartitionSpec as P

MESH = pl.DeviceIdType.MESH
F32 = jnp.float32
BF16 = jnp.bfloat16


def silu_pair(primal, tangent):
    sigma = jax.nn.sigmoid(primal)
    return primal * sigma, sigma * (1.0 + primal * (1.0 - sigma)) * tangent


class Links:
    def __init__(self, send_sems, recv_sems, count):
        self.send_sems, self.recv_sems, self.count = send_sems, recv_sems, count
        self.used = 0
        self.sent = []

    def copy(self, src, dst, device, slot=None):
        at = self.used
        self.used += 1
        assert self.used <= self.count
        desc = pltpu.make_async_remote_copy(
            src_ref=src,
            dst_ref=dst,
            send_sem=self.send_sems.at[at],
            recv_sem=self.recv_sems.at[at] if slot is None else slot,
            device_id=device,
            device_id_type=MESH,
        )
        return desc

    def start(self, src, dst, device):
        desc = self.copy(src, dst, device)
        desc.start()
        self.sent.append((None, desc))
        return desc

    def drain(self):
        for cond, desc in self.sent:
            if cond is None:
                desc.wait_send()
            else:
                pl.when(cond)(desc.wait_send)


class Ring:
    def __init__(self, links, view, at, to_z, up, down):
        self.links, self.view, self.to_z, self.up, self.down = links, view, to_z, up, down
        self.zh, self.a = at

    def send(self, z, a, to):
        view = self.view(z, a)
        return self.links.start(view, view, to)

    def start_z(self):
        self.z = self.send(self.zh, self.a, self.to_z)

    def start(self):
        self.own = self.send(self.zh, self.a, self.up), self.send(self.zh, self.a, self.down)

    def after_z(self):
        self.z.wait_recv()
        z = 1 - self.zh
        self.other = self.send(z, self.a, self.up), self.send(z, self.a, self.down)

    def forward(self):
        self.own[0].wait_recv()
        first = self.send(self.zh, (self.a + 3) % 4, self.up)
        self.other[1].wait_recv()
        self.far = first, self.send(1 - self.zh, (self.a + 1) % 4, self.down)

    def wait(self):
        for desc in (self.own[1], self.other[0]) + self.far:
            desc.wait_recv()


class Gather:
    def __init__(self, links, view, at, device, up, down):
        self.links, self.view, self.device, self.up, self.down = links, view, device, up, down
        self.zh, self.a, self.b = at
        self.near, self.first, self.second = {}, {}, {}

    def send(self, z, a, b, to):
        view = self.view(z, a, b)
        return self.links.start(view, view, to)

    def start(self):
        for da in (1, 3, 0, 2):
            for dz in range(2):
                if da or dz:
                    to = self.device((self.zh + dz) % 2, (self.a + da) % 4)
                    self.near[dz, da] = self.send(self.zh, self.a, self.b, to)

    def group(self, g):
        return (self.a + 4 - g) % 4

    def start_b(self, g):
        for dz in range(2):
            if g or dz:
                self.near[dz, g].wait_recv()
        a = self.group(g)
        self.first[g] = self.send(None, a, self.b, self.up), self.send(None, a, self.b, self.down)

    def forward_b(self, g):
        a = self.group(g)
        up, down = self.first[g]
        up.wait_recv()
        far = self.send(0, a, (self.b + 3) % 4, self.up)
        down.wait_recv()
        self.second[g] = far, self.send(1, a, (self.b + 1) % 4, self.down)

    def wait_b(self, g):
        for desc in self.second[g]:
            desc.wait_recv()


LINKS = 160
ORDER = (0, 1, 3, 2)


def kernel(
    fs, ft, wd32, wc32, wu32, out_s, out_t,
    ff, taps, wd_own, wd, wc, wu, part, part_in, first, first_z, mid, apad, acc, sums, sums_in,
    top, up_acc, spread, send_sems, recv_sems, mid_sems, plane_sems, sum_sems, local_sem,
):
    p = lax.axis_index("param")
    s = lax.axis_index("space")
    zl, c = p // 2, p % 2
    y, zh, x = s // 8, (s // 4) % 2, s % 4

    def space(yy, zz, xx):
        return 8 * yy + 4 * zz + xx

    sib = (2 * zl + 1 - c, s)
    across = (2 * (1 - zl) + c, s)
    swap = (2 * (1 - zl) + c, space((y + 2) % 4, zh, x))
    devs = {
        "zh": (p, space(y, 1 - zh, x)),
        "right": (p, space(y, zh, (x + 1) % 4)),
        "left": (p, space(y, zh, (x + 3) % 4)),
        "up": (p, space((y + 1) % 4, zh, x)),
        "down": (p, space((y + 3) % 4, zh, x)),
    }
    partners = [sib, across, swap]
    for dz in range(2):
        for da in range(4):
            if da or dz:
                partners.append((p, space(y, (zh + dz) % 2, (x + da) % 4)))
            if da:
                partners.append((p, space((y + da) % 4, (zh + dz) % 2, x)))
    barrier = pltpu.get_barrier_semaphore()
    for device in partners:
        pl.semaphore_signal(barrier, inc=1, device_id=device, device_id_type=MESH)

    placed = (y // 2) == zl
    wd_own[...] = wd32[...].astype(BF16)

    @pl.when(placed)
    def _():
        wd[y, zh, x] = wd_own[...]

    pl.semaphore_wait(barrier, len(partners))
    links = Links(send_sems, recv_sems, LINKS)

    moved = links.copy(wd_own, wd.at[(y + 2) % 4, zh, x], swap)
    links.sent.append((jnp.logical_not(placed), moved))
    pl.when(jnp.logical_not(placed))(moved.start)
    wc[zh, x] = wc32[...].astype(BF16)

    def pick(z):
        return slice(None) if z is None else z

    gd = (
        Gather(
            links, lambda z, a, b: wd.at[b, pick(z), a, 0:4], (zh, x, y),
            lambda z, a: (p, space(y, z, a)), devs["up"], devs["down"],
        ),
        Gather(
            links, lambda z, a, b: wd.at[a, pick(z), b, 4:8], (zh, y, x),
            lambda z, a: (p, space(a, z, x)), devs["right"], devs["left"],
        ),
    )
    gc = Ring(links, lambda z, a: wc.at[z, a], (zh, x), devs["zh"], devs["right"], devs["left"])
    gu = Gather(
        links, lambda z, a, b: wu.at[b, pick(z), a], (zh, x, y),
        lambda z, a: (p, space(y, z, a)), devs["up"], devs["down"],
    )
    pl.when(jnp.logical_not(placed))(moved.wait_recv)
    gd[0].start()
    gd[1].start()
    gc.start_z()

    def extract(f, fine):
        ff[...] = fine[...].astype(F32)
        for dz in range(2):
            for dy in range(2):
                for dx in range(2):
                    rows = ff[dz, :, dy, pl.ds(dx, 32, stride=2), :]
                    taps[c, 4 * dz + 2 * dy + dx, f] = rows.reshape(256, 128).astype(BF16)

    extract(0, fs)
    for g in ORDER:
        gd[0].start_b(g)
        gd[1].start_b(g)
    extract(1, ft)
    fine_copy = links.start(taps.at[c], taps.at[c], sib)
    for g in ORDER:
        gd[0].forward_b(g)
        gd[1].forward_b(g)
    gc.start()
    for t in range(4):
        for dx in range(2):
            wu[y, zh, x, t, :, 128 * dx : 128 * dx + 128] = wu32[2 * t + dx].astype(BF16)
    gu.start()
    gc.after_z()
    fine_copy.wait_recv()
    for g in ORDER:
        gd[0].wait_b(g)
        gd[1].wait_b(g)

    def down(half, h):
        total = None
        for t in range(8):
            rows = [taps[k, t, :, 128 * h : 128 * h + 128] for k in range(2)]
            rows = jnp.concatenate(rows, axis=-1).reshape(256, 256)
            weights = wd[pl.ds(2 * half, 2), :, :, t].reshape(256, 256)
            term = jnp.dot(rows, weights, preferred_element_type=F32)
            total = term if total is None else total + term
        return total

    part_copy = []
    for h in range(2):
        part[h] = down(1 - zl, h).astype(BF16)
        part_copy.append(links.start(part.at[h], part_in.at[h], across))
    for h in range(2):
        acc[h, :256] = down(zl, h)
    gc.forward()
    apad[:, :, pl.ds(0, 1)] = jnp.zeros((2, 6, 1, 32, 256), BF16)
    apad[:, :, pl.ds(9, 1)] = jnp.zeros((2, 6, 1, 32, 256), BF16)
    last_group = jnp.logical_and(x == 3, zh == 1)
    first_group = jnp.logical_and(x == 0, zh == 0)

    @pl.when(first_group)
    def _():
        apad[:, 0, pl.ds(1, 8)] = jnp.zeros((2, 8, 32, 256), BF16)

    @pl.when(last_group)
    def _():
        apad[:, 5, pl.ds(1, 8)] = jnp.zeros((2, 8, 32, 256), BF16)

    mids = {}

    def to_row(block, chunk, h):
        rows = pl.ds(4 * h, 4)
        move = links.copy(
            block.at[:, rows], mid.at[y, :, rows], (p, space(chunk, zh, x)), mid_sems.at[y, h]
        )
        away = chunk != y
        links.sent.append((away, move))
        pl.when(away)(move.start)

        @pl.when(chunk == y)
        def _():
            mid[y, :, rows] = block[:, rows]

    first_copy = []
    for h in range(2):
        part_copy[h].wait_recv()
        val, dir_ = silu_pair(
            acc[h, :128] + part_in[h, :128].astype(F32),
            acc[h, 128:256] + part_in[h, 128:].astype(F32),
        )
        rows = pl.ds(4 * h, 4)
        first[0, rows] = val.astype(BF16).reshape(4, 32, 256)
        first[1, rows] = dir_.astype(BF16).reshape(4, 32, 256)
        first_copy.append(links.start(first.at[:, rows], first_z.at[:, rows], across))
        to_row(first, p, h)
    for h in range(2):
        first_copy[h].wait_recv()
        to_row(first_z, 2 * (1 - zl) + c, h)

    gets = c == y % 2

    def window(slot, h):
        return apad.at[:, slot, pl.ds(1 + 4 * h, 4)]

    for h in range(2):
        for step in ORDER:
            source = (y + step) % 4
            block = mid.at[source, :, pl.ds(4 * h, 4)]
            if step:
                arrived = pltpu.make_async_remote_copy(
                    src_ref=block, dst_ref=block, send_sem=send_sems.at[0],
                    recv_sem=mid_sems.at[source, h], device_id=sib, device_id_type=MESH,
                )
                pl.when(gets)(arrived.wait_recv)
            stays = jnp.logical_and(gets, x == source)
            leaves = jnp.logical_and(gets, x != source)
            main = links.copy(
                block, window(x + 1, h), (p, space(y, zh, source)), plane_sems.at[x + 1, h]
            )
            links.sent.append((leaves, main))
            pl.when(leaves)(main.start)

            @pl.when(stays)
            def _():
                apad[:, x + 1, pl.ds(1 + 4 * h, 4)] = mid[source, :, pl.ds(4 * h, 4)]

            plane = space(source, zh, x)
            for slot, edge_x, group, end in (
                (0, 3, (plane + 1) // 4, 31), (5, 0, (plane + 31) // 4, 0)
            ):
                sends = jnp.logical_and(gets, jnp.logical_and(x == edge_x, plane != end))
                to = (p, space(y, group % 2, (group // 2) % 4))
                halo = links.copy(block, window(slot, h), to, plane_sems.at[slot, h])
                links.sent.append((sends, halo))
                pl.when(sends)(halo.start)
    gc.wait()

    for h in range(2):
        for slot in (1, 2, 3, 4, 0, 5):
            view = window(slot, h)
            hop = links.copy(view, view, sib, plane_sems.at[slot, h])
            sends = gets
            if slot == 0:
                arrives = jnp.logical_not(first_group)
                sends = jnp.logical_and(gets, arrives)
            elif slot == 5:
                arrives = jnp.logical_not(last_group)
                sends = jnp.logical_and(gets, arrives)
            else:
                arrives = jnp.logical_not(jnp.logical_and(gets, x == slot - 1))
            pl.when(arrives)(hop.wait_recv)
            links.sent.append((sends, hop))
            pl.when(sends)(hop.start)

    for g in ORDER:
        gu.start_b(g)

    edge = lax.broadcasted_iota(jnp.int32, (1, 32, 1), 1)
    for plane in range(4):
        for kx in range(3):
            total = None
            for kz in range(3):
                for ky in range(3):
                    rows = apad[:, plane + kz, ky : ky + 8].reshape(512, 256)
                    weights = wc[:, :, 9 * kz + 3 * ky + kx].reshape(256, 256)
                    term = jnp.dot(rows, weights, preferred_element_type=F32)
                    total = term if total is None else total + term
            acc[kx] = total
        low = pltpu.roll(acc[0], 1, 0).reshape(16, 32, 256)
        high = pltpu.roll(acc[2], 511, 0).reshape(16, 32, 256)
        total = acc[1].reshape(16, 32, 256)
        total = total + jnp.where(edge == 0, 0.0, low) + jnp.where(edge == 31, 0.0, high)
        sums[plane] = total.reshape(512, 256).astype(BF16)
        mine = jnp.logical_and(y == x, x == plane)
        away = jnp.logical_not(mine)
        part_sum = links.copy(
            sums.at[plane], sums_in.at[y], (p, space(x, zh, plane)), sum_sems.at[y]
        )
        links.sent.append((away, part_sum))
        pl.when(away)(part_sum.start)

        @pl.when(mine)
        def _():
            same = pltpu.make_async_copy(sums.at[plane], sums_in.at[y], local_sem)
            same.start()
            same.wait()

        gu.forward_b(ORDER[plane])

    for g in ORDER:
        gu.wait_b(g)
    for k in range(4):
        mine = jnp.logical_and(y == x, y == k)
        desc = pltpu.make_async_remote_copy(
            src_ref=sums.at[0], dst_ref=sums_in.at[k], send_sem=send_sems.at[0],
            recv_sem=sum_sems.at[k], device_id=sib, device_id_type=MESH,
        )
        pl.when(jnp.logical_not(mine))(desc.wait_recv)

    total = sums_in[0].astype(F32) + sums_in[1].astype(F32)
    total = total + (sums_in[2].astype(F32) + sums_in[3].astype(F32))
    val, dir_ = silu_pair(total[:256], total[256:])
    top[p, :256] = (val + first[0].reshape(256, 256).astype(F32)).astype(BF16)
    top[p, 256:] = (dir_ + first[1].reshape(256, 256).astype(F32)).astype(BF16)
    cross = links.start(top.at[p], top.at[p], across)
    near = links.start(top.at[p], top.at[p], sib)

    def add_up(chunk, fresh):
        rows = top[chunk]
        for t in range(4):
            weights = wu[chunk, :, :, t].reshape(256, 256)
            term = jnp.dot(rows, weights, preferred_element_type=F32)
            if fresh:
                up_acc[t] = term
            else:
                up_acc[t] += term

    add_up(p, True)
    near.wait_recv()
    add_up(sib[0], False)
    cross.wait_recv()
    relay = links.start(top.at[across[0]], top.at[across[0]], sib)
    add_up(across[0], False)
    relay.wait_recv()
    add_up(2 * (1 - zl) + 1 - c, False)
    for f, out in enumerate((out_s, out_t)):
        for t in range(4):
            for dx in range(2):
                block = up_acc[t, 256 * f : 256 * f + 256, 128 * dx : 128 * dx + 128]
                spread[t // 2, :, t % 2, pl.ds(dx, 32, stride=2), :] = block.reshape(8, 32, 128)
        out[...] = spread[...].astype(BF16)
    links.drain()


def local(fine_state, fine_tangent, down_weight, conv_weight, up_weight):
    vmem = pl.BlockSpec(memory_space=pltpu.VMEM)
    fine = (2, 8, 2, 64, 128)
    shape = jax.ShapeDtypeStruct(fine, BF16)
    state, tangent = pl.pallas_call(
        kernel,
        out_shape=(shape, shape),
        in_specs=[vmem] * 5,
        out_specs=(vmem, vmem),
        scratch_shapes=[
            pltpu.VMEM(fine, F32),
            pltpu.VMEM((2, 8, 2, 256, 128), BF16),
            pltpu.VMEM((8, 16, 256), BF16),
            pltpu.VMEM((4, 2, 4, 8, 16, 256), BF16),
            pltpu.VMEM((2, 4, 27, 32, 256), BF16),
            pltpu.VMEM((4, 2, 4, 4, 32, 256), BF16),
            pltpu.VMEM((2, 256, 256), BF16),
            pltpu.VMEM((2, 256, 256), BF16),
            pltpu.VMEM((2, 8, 32, 256), BF16),
            pltpu.VMEM((2, 8, 32, 256), BF16),
            pltpu.VMEM((4, 2, 8, 32, 256), BF16),
            pltpu.VMEM((2, 6, 10, 32, 256), BF16),
            pltpu.VMEM((3, 512, 256), F32),
            pltpu.VMEM((4, 512, 256), BF16),
            pltpu.VMEM((4, 512, 256), BF16),
            pltpu.VMEM((4, 512, 256), BF16),
            pltpu.VMEM((4, 512, 256), F32),
            pltpu.VMEM(fine, F32),
            pltpu.SemaphoreType.DMA((LINKS,)),
            pltpu.SemaphoreType.DMA((LINKS,)),
            pltpu.SemaphoreType.DMA((4, 2)),
            pltpu.SemaphoreType.DMA((6, 2)),
            pltpu.SemaphoreType.DMA((4,)),
            pltpu.SemaphoreType.DMA,
        ],
        compiler_params=pltpu.CompilerParams(
            collective_id=0, has_side_effects=True, vmem_limit_bytes=56 * 2**20
        ),
    )(fine_state.reshape(fine), fine_tangent.reshape(fine), down_weight, conv_weight, up_weight)
    return state.reshape(fine_state.shape), tangent.reshape(fine_state.shape)


def solution(mesh):
    in_specs = (
        P("space", None, None, "param"),
        P("space", None, None, "param"),
        P(None, "space", "param"),
        P(None, "space", "param"),
        P(None, "space", "param"),
    )
    out_specs = (P("space", None, None, "param"), P("space", None, None, "param"))
    return jax.shard_map(local, mesh=mesh, in_specs=in_specs, out_specs=out_specs, check_vma=False)
```

```python
import jax
import jax.numpy as jnp
from jax import lax
from jax.experimental import pallas as pl
from jax.experimental.pallas import tpu as pltpu
from jax.sharding import PartitionSpec as P

MESH = pl.DeviceIdType.MESH
F32 = jnp.float32
BF16 = jnp.bfloat16


def silu_gain(primal):
    sigma = jax.nn.sigmoid(primal)
    return primal * sigma, sigma * (1.0 + primal * (1.0 - sigma))


class Links:
    def __init__(self, send_sems, recv_sems, count):
        self.send_sems, self.recv_sems, self.count = send_sems, recv_sems, count
        self.used = 0
        self.sent = []

    def copy(self, src, dst, device, slot=None):
        at = self.used
        self.used += 1
        assert self.used <= self.count
        desc = pltpu.make_async_remote_copy(
            src_ref=src,
            dst_ref=dst,
            send_sem=self.send_sems.at[at],
            recv_sem=self.recv_sems.at[at] if slot is None else slot,
            device_id=device,
            device_id_type=MESH,
        )
        return desc

    def start(self, src, dst, device):
        desc = self.copy(src, dst, device)
        desc.start()
        self.sent.append((None, desc))
        return desc

    def drain(self):
        for cond, desc in self.sent:
            if cond is None:
                desc.wait_send()
            else:
                pl.when(cond)(desc.wait_send)


class Ring:
    def __init__(self, links, view, at, to_z, up, down):
        self.links, self.view, self.to_z, self.up, self.down = links, view, to_z, up, down
        self.zh, self.a = at

    def send(self, z, a, to):
        view = self.view(z, a)
        return self.links.start(view, view, to)

    def start_z(self):
        self.z = self.send(self.zh, self.a, self.to_z)

    def start(self):
        self.own = self.send(self.zh, self.a, self.up), self.send(self.zh, self.a, self.down)

    def after_z(self):
        self.z.wait_recv()
        z = 1 - self.zh
        self.other = self.send(z, self.a, self.up), self.send(z, self.a, self.down)

    def forward(self):
        self.own[0].wait_recv()
        first = self.send(self.zh, (self.a + 3) % 4, self.up)
        self.other[1].wait_recv()
        self.far = first, self.send(1 - self.zh, (self.a + 1) % 4, self.down)

    def wait(self):
        for desc in (self.own[1], self.other[0]) + self.far:
            desc.wait_recv()


class Gather:
    def __init__(self, links, view, at, to_z, to_a, up, down):
        self.links, self.view, self.up, self.down = links, view, up, down
        self.to_z, self.to_a = to_z, to_a
        self.zh, self.a, self.b = at
        self.near, self.first, self.second = {}, {}, {}

    def send(self, z, a, b, to):
        view = self.view(z, a, b)
        return self.links.start(view, view, to)

    def start(self):
        self.near[1, 0] = self.send(self.zh, self.a, self.b, self.to_z)
        for da in (1, 3, 2):
            self.near[0, da] = self.send(self.zh, self.a, self.b, self.to_a((self.a + da) % 4))

    def after_z(self):
        self.near[1, 0].wait_recv()
        for da in (1, 3, 2):
            self.near[1, da] = self.send(1 - self.zh, self.a, self.b, self.to_a((self.a + da) % 4))

    def group(self, g):
        return (self.a + 4 - g) % 4

    def start_b(self, g):
        if g:
            self.near[0, g].wait_recv()
            self.near[1, g].wait_recv()
        a = self.group(g)
        self.first[g] = self.send(None, a, self.b, self.up), self.send(None, a, self.b, self.down)

    def forward_b(self, g):
        a = self.group(g)
        up, down = self.first[g]
        up.wait_recv()
        far = self.send(0, a, (self.b + 3) % 4, self.up)
        down.wait_recv()
        self.second[g] = far, self.send(1, a, (self.b + 1) % 4, self.down)

    def wait_b(self, g):
        for desc in self.second[g]:
            desc.wait_recv()


LINKS = 160
SPLIT = 6
ORDER = (0, 1, 3, 2)


def kernel(
    fs, ft, wd32, wc32, wu32, out_s, out_t,
    ff, taps, wd_own, wd, wc, wu, part, part_in, first, first_z, mid, apad, acc, keep, sums, sums_in,
    top, up_acc, spread, send_sems, recv_sems, mid_sems, plane_sems, sum_sems,
):
    p = lax.axis_index("param")
    s = lax.axis_index("space")
    zl, c = p // 2, p % 2
    y, zh, x = s // 8, (s // 4) % 2, s % 4

    def space(yy, zz, xx):
        return 8 * yy + 4 * zz + xx

    sib = (2 * zl + 1 - c, s)
    across = (2 * (1 - zl) + c, s)
    swap = (2 * (1 - zl) + c, space((y + 2) % 4, zh, x))
    devs = {
        "zh": (p, space(y, 1 - zh, x)),
        "right": (p, space(y, zh, (x + 1) % 4)),
        "left": (p, space(y, zh, (x + 3) % 4)),
        "up": (p, space((y + 1) % 4, zh, x)),
        "down": (p, space((y + 3) % 4, zh, x)),
    }
    partners = [sib, across, swap]
    partners.append(devs["zh"])
    for step in range(1, 4):
        partners.append((p, space(y, zh, (x + step) % 4)))
        partners.append((p, space((y + step) % 4, zh, x)))
    barrier = pltpu.get_barrier_semaphore()
    for device in partners:
        pl.semaphore_signal(barrier, inc=1, device_id=device, device_id_type=MESH)

    placed = (y // 2) == zl
    wd_own[...] = wd32[...].astype(BF16)

    @pl.when(placed)
    def _():
        wd[y, zh, x] = wd_own[...]

    pl.semaphore_wait(barrier, len(partners))
    links = Links(send_sems, recv_sems, LINKS)

    moved = links.copy(wd_own, wd.at[(y + 2) % 4, zh, x], swap)
    links.sent.append((jnp.logical_not(placed), moved))
    pl.when(jnp.logical_not(placed))(moved.start)
    wc[zh, x] = wc32[...].astype(BF16)

    def pick(z):
        return slice(None) if z is None else z

    gd = (
        Gather(
            links, lambda z, a, b: wd.at[b, pick(z), a, :SPLIT], (zh, x, y),
            devs["zh"], lambda a: (p, space(y, zh, a)), devs["up"], devs["down"],
        ),
        Gather(
            links, lambda z, a, b: wd.at[a, pick(z), b, SPLIT:], (zh, y, x),
            devs["zh"], lambda a: (p, space(a, zh, x)), devs["right"], devs["left"],
        ),
    )
    gc = Ring(links, lambda z, a: wc.at[z, a], (zh, x), devs["zh"], devs["right"], devs["left"])
    gu = Gather(
        links, lambda z, a, b: wu.at[b, pick(z), a], (zh, x, y),
        devs["zh"], lambda a: (p, space(y, zh, a)), devs["up"], devs["down"],
    )
    gc.start_z()
    gc.start()

    for f, fine in enumerate((fs, ft)):
        ff[...] = fine[...].astype(F32)
        for dz in range(2):
            for dy in range(2):
                for dx in range(2):
                    rows = ff[dz, :, dy, pl.ds(dx, 32, stride=2), :]
                    taps[c, 4 * dz + 2 * dy + dx, f] = rows.reshape(256, 128).astype(BF16)
    fine_copy = links.start(taps.at[c], taps.at[c], sib)
    pl.when(jnp.logical_not(placed))(moved.wait_recv)
    for part_of in gd:
        part_of.start()
    for t in range(4):
        for dx in range(2):
            wu[y, zh, x, t, :, 128 * dx : 128 * dx + 128] = wu32[2 * t + dx].astype(BF16)
    for part_of in gd:
        part_of.after_z()
    for g in ORDER:
        gd[0].start_b(g)
        gd[1].start_b(g)
    gc.after_z()
    for g in ORDER:
        gd[0].forward_b(g)
        gd[1].forward_b(g)
    gu.start()
    gc.forward()
    fine_copy.wait_recv()
    for g in ORDER:
        gd[0].wait_b(g)
        gd[1].wait_b(g)

    def down(half, f):
        total = None
        for t in range(8):
            rows = jnp.concatenate([taps[0, t, f], taps[1, t, f]], axis=-1)
            weights = wd[pl.ds(2 * half, 2), :, :, t].reshape(256, 256)
            term = jnp.dot(rows, weights, preferred_element_type=F32)
            total = term if total is None else total + term
        return total

    part_copy = []
    for f in range(2):
        part[f] = down(1 - zl, f).astype(BF16)
        part_copy.append(links.start(part.at[f], part_in.at[f], across))
    for f in range(2):
        acc[f, :256] = down(zl, f)
    gu.after_z()
    apad[:, :, pl.ds(0, 1)] = jnp.zeros((2, 6, 1, 32, 256), BF16)
    apad[:, :, pl.ds(9, 1)] = jnp.zeros((2, 6, 1, 32, 256), BF16)
    last_group = jnp.logical_and(x == 3, zh == 1)
    first_group = jnp.logical_and(x == 0, zh == 0)

    @pl.when(first_group)
    def _():
        apad[:, 0, pl.ds(1, 8)] = jnp.zeros((2, 8, 32, 256), BF16)

    @pl.when(last_group)
    def _():
        apad[:, 5, pl.ds(1, 8)] = jnp.zeros((2, 8, 32, 256), BF16)

    def to_row(block, chunk, f):
        move = links.copy(
            block.at[f], mid.at[y, f], (p, space(chunk, zh, x)), mid_sems.at[y, f]
        )
        away = chunk != y
        links.sent.append((away, move))
        pl.when(away)(move.start)

        @pl.when(chunk == y)
        def _():
            mid[y, f] = block[f]

    first_copy = []
    for f in range(2):
        part_copy[f].wait_recv()
        pre = acc[f, :256] + part_in[f].astype(F32)
        if f == 0:
            value, gain = silu_gain(pre)
            acc[2, :256] = gain
        else:
            value = acc[2, :256] * pre
        first[f] = value.astype(BF16).reshape(8, 32, 256)
        first_copy.append(links.start(first.at[f], first_z.at[f], across))
        to_row(first, p, f)
    for f in range(2):
        first_copy[f].wait_recv()
        to_row(first_z, 2 * (1 - zl) + c, f)
    for g in ORDER:
        gu.start_b(g)

    gets = c == y % 2

    def window(slot, f):
        return apad.at[f, slot, pl.ds(1, 8)]

    def to_column(f):
        for step in ORDER:
            source = (y + step) % 4
            block = mid.at[source, f]
            if step:
                arrived = pltpu.make_async_remote_copy(
                    src_ref=block, dst_ref=block, send_sem=send_sems.at[0],
                    recv_sem=mid_sems.at[source, f], device_id=sib, device_id_type=MESH,
                )
                pl.when(gets)(arrived.wait_recv)
            stays = jnp.logical_and(gets, x == source)
            leaves = jnp.logical_and(gets, x != source)
            main = links.copy(
                block, window(x + 1, f), (p, space(y, zh, source)), plane_sems.at[x + 1, f]
            )
            links.sent.append((leaves, main))
            pl.when(leaves)(main.start)

            @pl.when(stays)
            def _():
                apad[f, x + 1, pl.ds(1, 8)] = mid[source, f]

            plane = space(source, zh, x)
            for slot, edge_x, group, end in (
                (0, 3, (plane + 1) // 4, 31), (5, 0, (plane + 31) // 4, 0)
            ):
                sends = jnp.logical_and(gets, jnp.logical_and(x == edge_x, plane != end))
                to = (p, space(y, group % 2, (group // 2) % 4))
                halo = links.copy(block, window(slot, f), to, plane_sems.at[slot, f])
                links.sent.append((sends, halo))
                pl.when(sends)(halo.start)

    def to_sibling(f):
        for slot in (1, 2, 3, 4, 0, 5):
            view = window(slot, f)
            hop = links.copy(view, view, sib, plane_sems.at[slot, f])
            sends = gets
            if slot == 0:
                arrives = jnp.logical_not(first_group)
                sends = jnp.logical_and(gets, arrives)
            elif slot == 5:
                arrives = jnp.logical_not(last_group)
                sends = jnp.logical_and(gets, arrives)
            else:
                arrives = jnp.logical_not(jnp.logical_and(gets, x == slot - 1))
            pl.when(arrives)(hop.wait_recv)
            links.sent.append((sends, hop))
            pl.when(sends)(hop.start)

    edge = lax.broadcasted_iota(jnp.int32, (1, 32, 1), 1)

    def convolve(f, pair):
        for kx in range(3):
            total = None
            for kz in range(3):
                for ky in range(3):
                    rows = apad[f, pl.ds(2 * pair + kz, 2), ky : ky + 8].reshape(512, 256)
                    weights = wc[:, :, 9 * kz + 3 * ky + kx].reshape(256, 256)
                    term = jnp.dot(rows, weights, preferred_element_type=F32)
                    total = term if total is None else total + term
            acc[kx] = total
        low = pltpu.roll(acc[0], 1, 0).reshape(16, 32, 256)
        high = pltpu.roll(acc[2], 511, 0).reshape(16, 32, 256)
        total = acc[1].reshape(16, 32, 256)
        total = total + jnp.where(edge == 0, 0.0, low) + jnp.where(edge == 31, 0.0, high)
        sums[f, pl.ds(2 * pair, 2)] = total.reshape(2, 256, 256).astype(BF16)
        for plane in (2 * pair, 2 * pair + 1):
            mine = jnp.logical_and(y == x, x == plane)
            away = jnp.logical_not(mine)
            move = links.copy(
                sums.at[f, plane], sums_in.at[f, y], (p, space(x, zh, plane)), sum_sems.at[f, y]
            )
            links.sent.append((away, move))
            pl.when(away)(move.start)

            @pl.when(mine)
            def _():
                sums_in[f, y] = sums[f, plane]

    def gather_sums(f):
        for k in range(4):
            mine = jnp.logical_and(y == x, y == k)
            desc = pltpu.make_async_remote_copy(
                src_ref=sums.at[f, 0], dst_ref=sums_in.at[f, k], send_sem=send_sems.at[0],
                recv_sem=sum_sems.at[f, k], device_id=sib, device_id_type=MESH,
            )
            pl.when(jnp.logical_not(mine))(desc.wait_recv)
        total = sums_in[f, 0].astype(F32) + sums_in[f, 1].astype(F32)
        return total + (sums_in[f, 2].astype(F32) + sums_in[f, 3].astype(F32))

    def send_top(f, value):
        top[p, f] = (value + first[f].reshape(256, 256).astype(F32)).astype(BF16)
        block = top.at[p, f]
        return links.start(block, block, across), links.start(block, block, sib)

    def relay_top(f, cross):
        cross.wait_recv()
        block = top.at[across[0], f]
        return links.start(block, block, sib)

    def add_up(f, chunk, fresh):
        rows = top[chunk, f]
        for t in range(4):
            weights = wu[chunk, :, :, t].reshape(256, 256)
            term = jnp.dot(rows, weights, preferred_element_type=F32)
            if fresh:
                up_acc[f, t] = term
            else:
                up_acc[f, t] += term

    def write(f, out):
        for t in range(4):
            for dx in range(2):
                block = up_acc[f, t, :, 128 * dx : 128 * dx + 128].reshape(8, 32, 128)
                spread[t // 2, :, t % 2, pl.ds(dx, 32, stride=2), :] = block
        out[...] = spread[...].astype(BF16)

    to_column(0)
    gc.wait()
    to_sibling(0)
    to_column(1)
    convolve(0, 0)
    convolve(0, 1)
    gu.forward_b(ORDER[0])
    gu.forward_b(ORDER[1])
    to_sibling(1)
    convolve(1, 0)
    value, gain = silu_gain(gather_sums(0))
    keep[...] = gain
    cross_0, near_0 = send_top(0, value)
    gu.forward_b(ORDER[2])
    gu.forward_b(ORDER[3])
    convolve(1, 1)
    relay_0 = relay_top(0, cross_0)
    for g in ORDER:
        gu.wait_b(g)
    add_up(0, p, True)
    cross_1, near_1 = send_top(1, keep[...] * gather_sums(1))
    near_0.wait_recv()
    add_up(0, sib[0], False)
    add_up(0, across[0], False)
    relay_0.wait_recv()
    add_up(0, 2 * (1 - zl) + 1 - c, False)
    write(0, out_s)
    add_up(1, p, True)
    near_1.wait_recv()
    add_up(1, sib[0], False)
    relay_1 = relay_top(1, cross_1)
    add_up(1, across[0], False)
    relay_1.wait_recv()
    add_up(1, 2 * (1 - zl) + 1 - c, False)
    write(1, out_t)
    links.drain()


def local(fine_state, fine_tangent, down_weight, conv_weight, up_weight):
    vmem = pl.BlockSpec(memory_space=pltpu.VMEM)
    fine = (2, 8, 2, 64, 128)
    shape = jax.ShapeDtypeStruct(fine, BF16)
    state, tangent = pl.pallas_call(
        kernel,
        out_shape=(shape, shape),
        in_specs=[vmem] * 5,
        out_specs=(vmem, vmem),
        scratch_shapes=[
            pltpu.VMEM(fine, F32),
            pltpu.VMEM((2, 8, 2, 256, 128), BF16),
            pltpu.VMEM((8, 16, 256), BF16),
            pltpu.VMEM((4, 2, 4, 8, 16, 256), BF16),
            pltpu.VMEM((2, 4, 27, 32, 256), BF16),
            pltpu.VMEM((4, 2, 4, 4, 32, 256), BF16),
            pltpu.VMEM((2, 256, 256), BF16),
            pltpu.VMEM((2, 256, 256), BF16),
            pltpu.VMEM((2, 8, 32, 256), BF16),
            pltpu.VMEM((2, 8, 32, 256), BF16),
            pltpu.VMEM((4, 2, 8, 32, 256), BF16),
            pltpu.VMEM((2, 6, 10, 32, 256), BF16),
            pltpu.VMEM((3, 512, 256), F32),
            pltpu.VMEM((256, 256), F32),
            pltpu.VMEM((2, 4, 256, 256), BF16),
            pltpu.VMEM((2, 4, 256, 256), BF16),
            pltpu.VMEM((4, 2, 256, 256), BF16),
            pltpu.VMEM((2, 4, 256, 256), F32),
            pltpu.VMEM(fine, F32),
            pltpu.SemaphoreType.DMA((LINKS,)),
            pltpu.SemaphoreType.DMA((LINKS,)),
            pltpu.SemaphoreType.DMA((4, 2)),
            pltpu.SemaphoreType.DMA((6, 2)),
            pltpu.SemaphoreType.DMA((2, 4)),
        ],
        compiler_params=pltpu.CompilerParams(
            collective_id=0, has_side_effects=True, vmem_limit_bytes=56 * 2**20
        ),
    )(fine_state.reshape(fine), fine_tangent.reshape(fine), down_weight, conv_weight, up_weight)
    return state.reshape(fine_state.shape), tangent.reshape(fine_state.shape)


def solution(mesh):
    in_specs = (
        P("space", None, None, "param"),
        P("space", None, None, "param"),
        P(None, "space", "param"),
        P(None, "space", "param"),
        P(None, "space", "param"),
    )
    out_specs = (P("space", None, None, "param"), P("space", None, None, "param"))
    return jax.shard_map(local, mesh=mesh, in_specs=in_specs, out_specs=out_specs, check_vma=False)
```

```python
import jax
import jax.numpy as jnp
from jax import lax
from jax.experimental import pallas as pl
from jax.experimental.pallas import tpu as pltpu
from jax.sharding import PartitionSpec as P

MESH = pl.DeviceIdType.MESH
F32 = jnp.float32
BF16 = jnp.bfloat16


def silu_gain(primal):
    sigma = jax.nn.sigmoid(primal)
    return primal * sigma, sigma * (1.0 + primal * (1.0 - sigma))


class Links:
    def __init__(self, send_sems, recv_sems, count):
        self.send_sems, self.recv_sems, self.count = send_sems, recv_sems, count
        self.used = 0
        self.sent = []

    def copy(self, src, dst, device, slot=None):
        at = self.used
        self.used += 1
        assert self.used <= self.count
        desc = pltpu.make_async_remote_copy(
            src_ref=src,
            dst_ref=dst,
            send_sem=self.send_sems.at[at],
            recv_sem=self.recv_sems.at[at] if slot is None else slot,
            device_id=device,
            device_id_type=MESH,
        )
        return desc

    def start(self, src, dst, device):
        desc = self.copy(src, dst, device)
        desc.start()
        self.sent.append((None, desc))
        return desc

    def drain(self):
        for cond, desc in self.sent:
            if cond is None:
                desc.wait_send()
            else:
                pl.when(cond)(desc.wait_send)


class Ring:
    def __init__(self, links, view, at, to_z, up, down):
        self.links, self.view, self.to_z, self.up, self.down = links, view, to_z, up, down
        self.zh, self.a = at

    def send(self, z, a, to):
        view = self.view(z, a)
        return self.links.start(view, view, to)

    def start_z(self):
        self.z = self.send(self.zh, self.a, self.to_z)

    def start(self):
        self.own = self.send(self.zh, self.a, self.up), self.send(self.zh, self.a, self.down)

    def after_z(self):
        self.z.wait_recv()
        z = 1 - self.zh
        self.other = self.send(z, self.a, self.up), self.send(z, self.a, self.down)

    def forward(self):
        self.own[0].wait_recv()
        first = self.send(self.zh, (self.a + 3) % 4, self.up)
        self.other[1].wait_recv()
        self.far = first, self.send(1 - self.zh, (self.a + 1) % 4, self.down)

    def wait(self):
        for desc in (self.own[1], self.other[0]) + self.far:
            desc.wait_recv()


class Gather:
    def __init__(self, links, view, at, to_z, to_a, up, down):
        self.links, self.view, self.up, self.down = links, view, up, down
        self.to_z, self.to_a = to_z, to_a
        self.zh, self.a, self.b = at
        self.near, self.first, self.second = {}, {}, {}

    def send(self, z, a, b, to):
        view = self.view(z, a, b)
        return self.links.start(view, view, to)

    def start(self):
        self.near[1, 0] = self.send(self.zh, self.a, self.b, self.to_z)
        for da in (1, 3, 2):
            self.near[0, da] = self.send(self.zh, self.a, self.b, self.to_a((self.a + da) % 4))

    def after_z(self):
        self.near[1, 0].wait_recv()
        for da in (1, 3, 2):
            self.near[1, da] = self.send(1 - self.zh, self.a, self.b, self.to_a((self.a + da) % 4))

    def group(self, g):
        return (self.a + 4 - g) % 4

    def start_b(self, g):
        if g:
            self.near[0, g].wait_recv()
            self.near[1, g].wait_recv()
        a = self.group(g)
        self.first[g] = self.send(None, a, self.b, self.up), self.send(None, a, self.b, self.down)

    def forward_b(self, g):
        a = self.group(g)
        up, down = self.first[g]
        up.wait_recv()
        far = self.send(0, a, (self.b + 3) % 4, self.up)
        down.wait_recv()
        self.second[g] = far, self.send(1, a, (self.b + 1) % 4, self.down)

    def wait_b(self, g):
        for desc in self.second[g]:
            desc.wait_recv()


LINKS = 192
SPLIT = 6
ORDER = (0, 1, 3, 2)


def kernel(
    fs, ft, wd32, wc32, wu32, out_s, out_t,
    ff, taps, wd_own, wd, wc, wu, part, part_in, first, first_z, mid, apad, acc, keep, sums, sums_in,
    top, up_acc, spread, fine_out, send_sems, recv_sems, mid_sems, plane_sems, sum_sems, out_sems,
):
    p = lax.axis_index("param")
    s = lax.axis_index("space")
    zl, c = p // 2, p % 2
    y, zh, x = s // 8, (s // 4) % 2, s % 4

    def space(yy, zz, xx):
        return 8 * yy + 4 * zz + xx

    sib = (2 * zl + 1 - c, s)
    across = (2 * (1 - zl) + c, s)
    swap = (2 * (1 - zl) + c, space((y + 2) % 4, zh, x))
    devs = {
        "zh": (p, space(y, 1 - zh, x)),
        "right": (p, space(y, zh, (x + 1) % 4)),
        "left": (p, space(y, zh, (x + 3) % 4)),
        "up": (p, space((y + 1) % 4, zh, x)),
        "down": (p, space((y + 3) % 4, zh, x)),
    }
    partners = [sib, across, swap]
    partners.append(devs["zh"])
    for step in range(1, 4):
        partners.append((p, space(y, zh, (x + step) % 4)))
        partners.append((p, space((y + step) % 4, zh, x)))
    barrier = pltpu.get_barrier_semaphore()
    for device in partners:
        pl.semaphore_signal(barrier, inc=1, device_id=device, device_id_type=MESH)

    placed = (y // 2) == zl
    wd_own[...] = wd32[...].astype(BF16)

    @pl.when(placed)
    def _():
        wd[y, zh, x] = wd_own[...]

    pl.semaphore_wait(barrier, len(partners))
    links = Links(send_sems, recv_sems, LINKS)

    moved = links.copy(wd_own, wd.at[(y + 2) % 4, zh, x], swap)
    links.sent.append((jnp.logical_not(placed), moved))
    pl.when(jnp.logical_not(placed))(moved.start)
    wc[zh, x] = wc32[...].astype(BF16)

    def pick(z):
        return slice(None) if z is None else z

    gd = (
        Gather(
            links, lambda z, a, b: wd.at[b, pick(z), a, :SPLIT], (zh, x, y),
            devs["zh"], lambda a: (p, space(y, zh, a)), devs["up"], devs["down"],
        ),
        Gather(
            links, lambda z, a, b: wd.at[a, pick(z), b, SPLIT:], (zh, y, x),
            devs["zh"], lambda a: (p, space(a, zh, x)), devs["right"], devs["left"],
        ),
    )
    gc = Ring(links, lambda z, a: wc.at[z, a], (zh, x), devs["zh"], devs["right"], devs["left"])
    gu = Gather(
        links, lambda z, a, b: wu.at[b, pick(z), a], (zh, x, y),
        devs["zh"], lambda a: (p, space(y, zh, a)), devs["up"], devs["down"],
    )
    gc.start_z()
    gc.start()

    for f, fine in enumerate((fs, ft)):
        ff[...] = fine[...].astype(F32)
        for dz in range(2):
            for dy in range(2):
                for dx in range(2):
                    rows = ff[dz, :, dy, pl.ds(dx, 32, stride=2), :]
                    taps[c, 4 * dz + 2 * dy + dx, f] = rows.reshape(256, 128).astype(BF16)
    fine_copy = links.start(taps.at[c], taps.at[c], sib)
    pl.when(jnp.logical_not(placed))(moved.wait_recv)
    for part_of in gd:
        part_of.start()
    for t in range(4):
        for dx in range(2):
            wu[y, zh, x, t, :, 128 * dx : 128 * dx + 128] = wu32[2 * t + dx].astype(BF16)
    for part_of in gd:
        part_of.after_z()
    for g in ORDER:
        gd[0].start_b(g)
        gd[1].start_b(g)
    gc.after_z()
    for g in ORDER:
        gd[0].forward_b(g)
        gd[1].forward_b(g)
    gu.start()
    gc.forward()
    fine_copy.wait_recv()
    for g in ORDER:
        gd[0].wait_b(g)
        gd[1].wait_b(g)

    def down(half, f):
        total = None
        for t in range(8):
            rows = jnp.concatenate([taps[0, t, f], taps[1, t, f]], axis=-1)
            weights = wd[pl.ds(2 * half, 2), :, :, t].reshape(256, 256)
            term = jnp.dot(rows, weights, preferred_element_type=F32)
            total = term if total is None else total + term
        return total

    part_copy = []
    for f in range(2):
        for own in range(2):
            other = down(1 - zl, f) if own == 0 else down(zl, f)
            acc[f, 256 * (1 - own) : 256 * (2 - own)] = other
            part[f, own] = other.astype(BF16)
            part_copy.append(links.start(part.at[f, own], part_in.at[f, own], across))
    gu.after_z()
    apad[:, :, pl.ds(0, 1)] = jnp.zeros((2, 6, 1, 32, 256), BF16)
    apad[:, :, pl.ds(9, 1)] = jnp.zeros((2, 6, 1, 32, 256), BF16)
    last_group = jnp.logical_and(x == 3, zh == 1)
    first_group = jnp.logical_and(x == 0, zh == 0)

    @pl.when(first_group)
    def _():
        apad[:, 0, pl.ds(1, 8)] = jnp.zeros((2, 8, 32, 256), BF16)

    @pl.when(last_group)
    def _():
        apad[:, 5, pl.ds(1, 8)] = jnp.zeros((2, 8, 32, 256), BF16)

    def to_row(block, chunk, f):
        move = links.copy(
            block.at[f], mid.at[y, f], (p, space(chunk, zh, x)), mid_sems.at[y, f]
        )
        away = chunk != y
        links.sent.append((away, move))
        pl.when(away)(move.start)

        @pl.when(chunk == y)
        def _():
            mid[y, f] = block[f]

    for f in range(2):
        for k, block in enumerate((first, first_z)):
            part_copy[2 * f + k].wait_recv()
            pre = acc[f, 256 * k : 256 * k + 256] + part_in[f, k].astype(F32)
            if f == 0:
                value, gain = silu_gain(pre)
                acc[2, 256 * k : 256 * k + 256] = gain
            else:
                value = acc[2, 256 * k : 256 * k + 256] * pre
            block[f] = value.astype(BF16).reshape(8, 32, 256)
            to_row(block, across[0] if k else p, f)
    for g in ORDER:
        gu.start_b(g)

    gets = c == y % 2

    def window(slot, f):
        return apad.at[f, slot, pl.ds(1, 8)]

    def to_column(f):
        for step in ORDER:
            source = (y + step) % 4
            block = mid.at[source, f]
            if step:
                arrived = pltpu.make_async_remote_copy(
                    src_ref=block, dst_ref=block, send_sem=send_sems.at[0],
                    recv_sem=mid_sems.at[source, f], device_id=sib, device_id_type=MESH,
                )
                pl.when(gets)(arrived.wait_recv)
            stays = jnp.logical_and(gets, x == source)
            leaves = jnp.logical_and(gets, x != source)
            main = links.copy(
                block, window(x + 1, f), (p, space(y, zh, source)), plane_sems.at[x + 1, f]
            )
            links.sent.append((leaves, main))
            pl.when(leaves)(main.start)

            @pl.when(stays)
            def _():
                apad[f, x + 1, pl.ds(1, 8)] = mid[source, f]

            plane = space(source, zh, x)
            for slot, edge_x, group, end in (
                (0, 3, (plane + 1) // 4, 31), (5, 0, (plane + 31) // 4, 0)
            ):
                sends = jnp.logical_and(gets, jnp.logical_and(x == edge_x, plane != end))
                to = (p, space(y, group % 2, (group // 2) % 4))
                halo = links.copy(block, window(slot, f), to, plane_sems.at[slot, f])
                links.sent.append((sends, halo))
                pl.when(sends)(halo.start)

    def to_sibling(f):
        for slot in (1, 2, 3, 4, 0, 5):
            view = window(slot, f)
            hop = links.copy(view, view, sib, plane_sems.at[slot, f])
            sends = gets
            if slot == 0:
                arrives = jnp.logical_not(first_group)
                sends = jnp.logical_and(gets, arrives)
            elif slot == 5:
                arrives = jnp.logical_not(last_group)
                sends = jnp.logical_and(gets, arrives)
            else:
                arrives = jnp.logical_not(jnp.logical_and(gets, x == slot - 1))
            pl.when(arrives)(hop.wait_recv)
            links.sent.append((sends, hop))
            pl.when(sends)(hop.start)

    edge = lax.broadcasted_iota(jnp.int32, (1, 32, 1), 1)

    def convolve(f, h):
        for kx in range(3):
            total = None
            for kz in range(3):
                for ky in range(3):
                    rows = apad[f, kz : kz + 4, 4 * h + ky : 4 * h + ky + 4].reshape(512, 256)
                    weights = wc[:, :, 9 * kz + 3 * ky + kx].reshape(256, 256)
                    term = jnp.dot(rows, weights, preferred_element_type=F32)
                    total = term if total is None else total + term
            acc[kx] = total
        low = pltpu.roll(acc[0], 1, 0).reshape(16, 32, 256)
        high = pltpu.roll(acc[2], 511, 0).reshape(16, 32, 256)
        total = acc[1].reshape(16, 32, 256)
        total = total + jnp.where(edge == 0, 0.0, low) + jnp.where(edge == 31, 0.0, high)
        sums[f, h] = total.reshape(4, 128, 256).astype(BF16)
        for plane in range(4):
            mine = jnp.logical_and(y == x, x == plane)
            away = jnp.logical_not(mine)
            move = links.copy(
                sums.at[f, h, plane], sums_in.at[f, h, y], (p, space(x, zh, plane)),
                sum_sems.at[2 * f + h, y],
            )
            links.sent.append((away, move))
            pl.when(away)(move.start)

            @pl.when(mine)
            def _():
                sums_in[f, h, y] = sums[f, h, plane]

    def gather_sums(f, h):
        for k in range(4):
            mine = jnp.logical_and(y == x, y == k)
            desc = pltpu.make_async_remote_copy(
                src_ref=sums.at[f, h, 0], dst_ref=sums_in.at[f, h, k], send_sem=send_sems.at[0],
                recv_sem=sum_sems.at[2 * f + h, k], device_id=sib, device_id_type=MESH,
            )
            pl.when(jnp.logical_not(mine))(desc.wait_recv)
        total = sums_in[f, h, 0].astype(F32) + sums_in[f, h, 1].astype(F32)
        return total + (sums_in[f, h, 2].astype(F32) + sums_in[f, h, 3].astype(F32))

    def send_top(f, h, value):
        skip = first[f, 4 * h : 4 * h + 4].reshape(128, 256).astype(F32)
        top[p, f, h] = (value + skip).astype(BF16)
        block = top.at[p, f, h]
        return links.start(block, block, across), links.start(block, block, sib)

    def relay_top(f, h, cross):
        cross.wait_recv()
        block = top.at[across[0], f, h]
        return links.start(block, block, sib)

    def add_up(f, chunk, fresh):
        rows = top[chunk, f].reshape(256, 256)
        for t in range(4):
            weights = wu[chunk, :, :, t].reshape(256, 256)
            term = jnp.dot(rows, weights, preferred_element_type=F32)
            if fresh:
                up_acc[f, t] = term
            else:
                up_acc[f, t] += term

    def write(f, out):
        for t in range(4):
            for dx in range(2):
                block = up_acc[f, t, :, 128 * dx : 128 * dx + 128].reshape(8, 32, 128)
                spread[t // 2, :, t % 2, pl.ds(dx, 32, stride=2), :] = block
        fine_out[f] = spread[...].astype(BF16)
        move = pltpu.make_async_copy(fine_out.at[f], out, out_sems.at[f])
        move.start()
        return move

    last = 2 * (1 - zl) + 1 - c
    to_column(0)
    gc.wait()
    to_sibling(0)
    to_column(1)
    convolve(0, 0)
    convolve(0, 1)
    gu.forward_b(ORDER[0])
    gu.forward_b(ORDER[1])
    to_sibling(1)
    convolve(1, 0)
    state = []
    for h in range(2):
        value, gain = silu_gain(gather_sums(0, h))
        keep[h] = gain
        state.append(send_top(0, h, value))
    gu.forward_b(ORDER[2])
    gu.forward_b(ORDER[3])
    convolve(1, 1)
    relays = [relay_top(0, h, state[h][0]) for h in range(2)]
    tangent = [send_top(1, 0, keep[0] * gather_sums(1, 0))]
    for g in ORDER:
        gu.wait_b(g)
    add_up(0, p, True)
    tangent.append(send_top(1, 1, keep[1] * gather_sums(1, 1)))
    for h in range(2):
        state[h][1].wait_recv()
    add_up(0, sib[0], False)
    add_up(0, across[0], False)
    for h in range(2):
        relays[h].wait_recv()
    add_up(0, last, False)
    relays = [relay_top(1, 0, tangent[0][0])]
    moves = [write(0, out_s)]
    add_up(1, p, True)
    relays.append(relay_top(1, 1, tangent[1][0]))
    for h in range(2):
        tangent[h][1].wait_recv()
    add_up(1, sib[0], False)
    add_up(1, across[0], False)
    for h in range(2):
        relays[h].wait_recv()
    add_up(1, last, False)
    moves.append(write(1, out_t))
    for move in moves:
        move.wait()
    links.drain()


def local(fine_state, fine_tangent, down_weight, conv_weight, up_weight):
    vmem = pl.BlockSpec(memory_space=pltpu.VMEM)
    whole = pl.BlockSpec(memory_space=pl.ANY)
    fine = (2, 8, 2, 64, 128)
    shape = jax.ShapeDtypeStruct(fine, BF16)
    state, tangent = pl.pallas_call(
        kernel,
        out_shape=(shape, shape),
        in_specs=[vmem] * 5,
        out_specs=(whole, whole),
        scratch_shapes=[
            pltpu.VMEM(fine, F32),
            pltpu.VMEM((2, 8, 2, 256, 128), BF16),
            pltpu.VMEM((8, 16, 256), BF16),
            pltpu.VMEM((4, 2, 4, 8, 16, 256), BF16),
            pltpu.VMEM((2, 4, 27, 32, 256), BF16),
            pltpu.VMEM((4, 2, 4, 4, 32, 256), BF16),
            pltpu.VMEM((2, 2, 256, 256), BF16),
            pltpu.VMEM((2, 2, 256, 256), BF16),
            pltpu.VMEM((2, 8, 32, 256), BF16),
            pltpu.VMEM((2, 8, 32, 256), BF16),
            pltpu.VMEM((4, 2, 8, 32, 256), BF16),
            pltpu.VMEM((2, 6, 10, 32, 256), BF16),
            pltpu.VMEM((3, 512, 256), F32),
            pltpu.VMEM((2, 128, 256), F32),
            pltpu.VMEM((2, 2, 4, 128, 256), BF16),
            pltpu.VMEM((2, 2, 4, 128, 256), BF16),
            pltpu.VMEM((4, 2, 2, 128, 256), BF16),
            pltpu.VMEM((2, 4, 256, 256), F32),
            pltpu.VMEM(fine, F32),
            pltpu.VMEM((2,) + fine, BF16),
            pltpu.SemaphoreType.DMA((LINKS,)),
            pltpu.SemaphoreType.DMA((LINKS,)),
            pltpu.SemaphoreType.DMA((4, 2)),
            pltpu.SemaphoreType.DMA((6, 2)),
            pltpu.SemaphoreType.DMA((4, 4)),
            pltpu.SemaphoreType.DMA((2,)),
        ],
        compiler_params=pltpu.CompilerParams(
            collective_id=0, has_side_effects=True, vmem_limit_bytes=56 * 2**20
        ),
    )(fine_state.reshape(fine), fine_tangent.reshape(fine), down_weight, conv_weight, up_weight)
    return state.reshape(fine_state.shape), tangent.reshape(fine_state.shape)


def solution(mesh):
    in_specs = (
        P("space", None, None, "param"),
        P("space", None, None, "param"),
        P(None, "space", "param"),
        P(None, "space", "param"),
        P(None, "space", "param"),
    )
    out_specs = (P("space", None, None, "param"), P("space", None, None, "param"))
    return jax.shard_map(local, mesh=mesh, in_specs=in_specs, out_specs=out_specs, check_vma=False)
```

```python
import jax
import jax.numpy as jnp
from jax import lax
from jax.experimental import pallas as pl
from jax.experimental.pallas import tpu as pltpu
from jax.sharding import PartitionSpec as P

MESH = pl.DeviceIdType.MESH
F32 = jnp.float32
BF16 = jnp.bfloat16


def silu_gain(primal):
    sigma = jax.nn.sigmoid(primal)
    return primal * sigma, sigma * (1.0 + primal * (1.0 - sigma))


class Links:
    def __init__(self, send_sems, recv_sems, count):
        self.send_sems, self.recv_sems, self.count = send_sems, recv_sems, count
        self.used = 0
        self.sent = []

    def copy(self, src, dst, device, slot=None):
        at = self.used
        self.used += 1
        assert self.used <= self.count
        desc = pltpu.make_async_remote_copy(
            src_ref=src,
            dst_ref=dst,
            send_sem=self.send_sems.at[at],
            recv_sem=self.recv_sems.at[at] if slot is None else slot,
            device_id=device,
            device_id_type=MESH,
        )
        return desc

    def start(self, src, dst, device):
        desc = self.copy(src, dst, device)
        desc.start()
        self.sent.append((None, desc))
        return desc

    def drain(self):
        for cond, desc in self.sent:
            if cond is None:
                desc.wait_send()
            else:
                pl.when(cond)(desc.wait_send)


class Ring:
    def __init__(self, links, view, at, to_z, up, down):
        self.links, self.view, self.to_z, self.up, self.down = links, view, to_z, up, down
        self.zh, self.a = at

    def send(self, z, a, to):
        view = self.view(z, a)
        return self.links.start(view, view, to)

    def start_z(self):
        self.z = self.send(self.zh, self.a, self.to_z)

    def start(self):
        self.own = self.send(self.zh, self.a, self.up), self.send(self.zh, self.a, self.down)

    def after_z(self):
        self.z.wait_recv()
        z = 1 - self.zh
        self.other = self.send(z, self.a, self.up), self.send(z, self.a, self.down)

    def forward(self):
        self.own[0].wait_recv()
        first = self.send(self.zh, (self.a + 3) % 4, self.up)
        self.other[1].wait_recv()
        self.far = first, self.send(1 - self.zh, (self.a + 1) % 4, self.down)

    def wait(self):
        for desc in (self.own[1], self.other[0]) + self.far:
            desc.wait_recv()


class Gather:
    def __init__(self, links, view, at, to_z, to_a, up, down):
        self.links, self.view, self.up, self.down = links, view, up, down
        self.to_z, self.to_a = to_z, to_a
        self.zh, self.a, self.b = at
        self.near, self.first, self.second = {}, {}, {}

    def send(self, z, a, b, to):
        view = self.view(z, a, b)
        return self.links.start(view, view, to)

    def start(self):
        self.near[1, 0] = self.send(self.zh, self.a, self.b, self.to_z)
        for da in (1, 3, 2):
            self.near[0, da] = self.send(self.zh, self.a, self.b, self.to_a((self.a + da) % 4))

    def after_z(self):
        self.near[1, 0].wait_recv()
        for da in (1, 3, 2):
            self.near[1, da] = self.send(1 - self.zh, self.a, self.b, self.to_a((self.a + da) % 4))

    def group(self, g):
        return (self.a + 4 - g) % 4

    def start_b(self, g):
        if g:
            self.near[0, g].wait_recv()
            self.near[1, g].wait_recv()
        a = self.group(g)
        self.first[g] = self.send(None, a, self.b, self.up), self.send(None, a, self.b, self.down)

    def forward_b(self, g):
        a = self.group(g)
        up, down = self.first[g]
        up.wait_recv()
        far = self.send(0, a, (self.b + 3) % 4, self.up)
        down.wait_recv()
        self.second[g] = far, self.send(1, a, (self.b + 1) % 4, self.down)

    def wait_b(self, g):
        for desc in self.second[g]:
            desc.wait_recv()


LINKS = 192
SPLIT = 7
ORDER = (0, 1, 3, 2)


def kernel(
    fs, ft, wd32, wc_in, wu_in, out_s, out_t,
    fine_in, wc32, wu32,
    ff, taps, wd_own, wd, wc, wu, part, part_in, first, first_z, mid, apad, acc, keep, sums, sums_in,
    top, up_acc, spread, fine_out, send_sems, recv_sems, mid_sems, plane_sems, sum_sems, out_sems, in_sems,
):
    loads = []
    for at, (src, dst) in enumerate(
        ((wc_in, wc32), (fs, fine_in.at[0]), (ft, fine_in.at[1]), (wu_in, wu32))
    ):
        loads.append(pltpu.make_async_copy(src, dst, in_sems.at[at]))
        loads[-1].start()
    p = lax.axis_index("param")
    s = lax.axis_index("space")
    zl, c = p // 2, p % 2
    y, zh, x = s // 8, (s // 4) % 2, s % 4

    def space(yy, zz, xx):
        return 8 * yy + 4 * zz + xx

    sib = (2 * zl + 1 - c, s)
    across = (2 * (1 - zl) + c, s)
    swap = (2 * (1 - zl) + c, space((y + 2) % 4, zh, x))
    devs = {
        "zh": (p, space(y, 1 - zh, x)),
        "right": (p, space(y, zh, (x + 1) % 4)),
        "left": (p, space(y, zh, (x + 3) % 4)),
        "up": (p, space((y + 1) % 4, zh, x)),
        "down": (p, space((y + 3) % 4, zh, x)),
    }
    partners = [sib, across, swap]
    partners.append(devs["zh"])
    for step in range(1, 4):
        partners.append((p, space(y, zh, (x + step) % 4)))
        partners.append((p, space((y + step) % 4, zh, x)))
    barrier = pltpu.get_barrier_semaphore()
    for device in partners:
        pl.semaphore_signal(barrier, inc=1, device_id=device, device_id_type=MESH)

    placed = (y // 2) == zl
    wd_own[...] = wd32[...].astype(BF16)

    @pl.when(placed)
    def _():
        wd[y, zh, x] = wd_own[...]

    pl.semaphore_wait(barrier, len(partners))
    links = Links(send_sems, recv_sems, LINKS)

    moved = links.copy(wd_own, wd.at[(y + 2) % 4, zh, x], swap)
    links.sent.append((jnp.logical_not(placed), moved))
    pl.when(jnp.logical_not(placed))(moved.start)
    loads[0].wait()
    wc[zh, x] = wc32[...].astype(BF16)

    def pick(z):
        return slice(None) if z is None else z

    gd = (
        Gather(
            links, lambda z, a, b: wd.at[b, pick(z), a, :SPLIT], (zh, x, y),
            devs["zh"], lambda a: (p, space(y, zh, a)), devs["up"], devs["down"],
        ),
        Gather(
            links, lambda z, a, b: wd.at[a, pick(z), b, SPLIT:], (zh, y, x),
            devs["zh"], lambda a: (p, space(a, zh, x)), devs["right"], devs["left"],
        ),
    )
    gc = Ring(links, lambda z, a: wc.at[z, a], (zh, x), devs["zh"], devs["right"], devs["left"])
    gu = Gather(
        links, lambda z, a, b: wu.at[b, pick(z), a], (zh, x, y),
        devs["zh"], lambda a: (p, space(y, zh, a)), devs["up"], devs["down"],
    )
    gc.start()

    for f in range(2):
        loads[1 + f].wait()
        ff[...] = fine_in[f].astype(F32)
        for dz in range(2):
            for dy in range(2):
                for dx in range(2):
                    rows = ff[dz, :, dy, pl.ds(dx, 32, stride=2), :]
                    taps[c, 4 * dz + 2 * dy + dx, f] = rows.reshape(256, 128).astype(BF16)
    fine_copy = links.start(taps.at[c], taps.at[c], sib)
    pl.when(jnp.logical_not(placed))(moved.wait_recv)
    for part_of in gd:
        part_of.start()
    gc.start_z()
    loads[3].wait()
    for t in range(4):
        for dx in range(2):
            wu[y, zh, x, t, :, 128 * dx : 128 * dx + 128] = wu32[2 * t + dx].astype(BF16)
    for part_of in gd:
        part_of.after_z()
    for g in ORDER:
        gd[0].start_b(g)
        gd[1].start_b(g)
    gc.after_z()
    for g in ORDER:
        gd[0].forward_b(g)
        gd[1].forward_b(g)
    gu.start()
    gc.forward()
    fine_copy.wait_recv()
    for g in ORDER:
        gd[0].wait_b(g)
        gd[1].wait_b(g)

    def down(half, f):
        total = None
        for t in range(8):
            rows = jnp.concatenate([taps[0, t, f], taps[1, t, f]], axis=-1)
            weights = wd[pl.ds(2 * half, 2), :, :, t].reshape(256, 256)
            term = jnp.dot(rows, weights, preferred_element_type=F32)
            total = term if total is None else total + term
        return total

    part_copy = []
    for f in range(2):
        for own in range(2):
            other = down(1 - zl, f) if own == 0 else down(zl, f)
            acc[f, 256 * (1 - own) : 256 * (2 - own)] = other
            part[f, own] = other.astype(BF16)
            part_copy.append(links.start(part.at[f, own], part_in.at[f, own], across))
    gu.after_z()
    apad[:, :, pl.ds(0, 1)] = jnp.zeros((2, 6, 1, 32, 256), BF16)
    apad[:, :, pl.ds(9, 1)] = jnp.zeros((2, 6, 1, 32, 256), BF16)
    last_group = jnp.logical_and(x == 3, zh == 1)
    first_group = jnp.logical_and(x == 0, zh == 0)

    @pl.when(first_group)
    def _():
        apad[:, 0, pl.ds(1, 8)] = jnp.zeros((2, 8, 32, 256), BF16)

    @pl.when(last_group)
    def _():
        apad[:, 5, pl.ds(1, 8)] = jnp.zeros((2, 8, 32, 256), BF16)

    def to_row(block, chunk, f):
        move = links.copy(
            block.at[f], mid.at[y, f], (p, space(chunk, zh, x)), mid_sems.at[y, f]
        )
        away = chunk != y
        links.sent.append((away, move))
        pl.when(away)(move.start)

        @pl.when(chunk == y)
        def _():
            mid[y, f] = block[f]

    for f in range(2):
        for k, block in enumerate((first, first_z)):
            part_copy[2 * f + k].wait_recv()
            pre = acc[f, 256 * k : 256 * k + 256] + part_in[f, k].astype(F32)
            if f == 0:
                value, gain = silu_gain(pre)
                acc[2, 256 * k : 256 * k + 256] = gain
            else:
                value = acc[2, 256 * k : 256 * k + 256] * pre
            block[f] = value.astype(BF16).reshape(8, 32, 256)
            to_row(block, across[0] if k else p, f)
    for g in ORDER:
        gu.start_b(g)

    gets = c == y % 2

    def window(slot, f):
        return apad.at[f, slot, pl.ds(1, 8)]

    def to_column(f):
        for step in ORDER:
            source = (y + step) % 4
            block = mid.at[source, f]
            if step:
                arrived = pltpu.make_async_remote_copy(
                    src_ref=block, dst_ref=block, send_sem=send_sems.at[0],
                    recv_sem=mid_sems.at[source, f], device_id=sib, device_id_type=MESH,
                )
                pl.when(gets)(arrived.wait_recv)
            stays = jnp.logical_and(gets, x == source)
            leaves = jnp.logical_and(gets, x != source)
            main = links.copy(
                block, window(x + 1, f), (p, space(y, zh, source)), plane_sems.at[x + 1, f]
            )
            links.sent.append((leaves, main))
            pl.when(leaves)(main.start)

            @pl.when(stays)
            def _():
                apad[f, x + 1, pl.ds(1, 8)] = mid[source, f]

            plane = space(source, zh, x)
            for slot, edge_x, group, end in (
                (0, 3, (plane + 1) // 4, 31), (5, 0, (plane + 31) // 4, 0)
            ):
                sends = jnp.logical_and(gets, jnp.logical_and(x == edge_x, plane != end))
                to = (p, space(y, group % 2, (group // 2) % 4))
                halo = links.copy(block, window(slot, f), to, plane_sems.at[slot, f])
                links.sent.append((sends, halo))
                pl.when(sends)(halo.start)

    def to_sibling(f):
        for slot in (1, 2, 3, 4, 0, 5):
            view = window(slot, f)
            hop = links.copy(view, view, sib, plane_sems.at[slot, f])
            sends = gets
            if slot == 0:
                arrives = jnp.logical_not(first_group)
                sends = jnp.logical_and(gets, arrives)
            elif slot == 5:
                arrives = jnp.logical_not(last_group)
                sends = jnp.logical_and(gets, arrives)
            else:
                arrives = jnp.logical_not(jnp.logical_and(gets, x == slot - 1))
            pl.when(arrives)(hop.wait_recv)
            links.sent.append((sends, hop))
            pl.when(sends)(hop.start)

    edge = lax.broadcasted_iota(jnp.int32, (1, 32, 1), 1)

    def convolve(f, h):
        for kx in range(3):
            total = None
            for kz in range(3):
                for ky in range(3):
                    rows = apad[f, kz : kz + 4, 4 * h + ky : 4 * h + ky + 4].reshape(512, 256)
                    weights = wc[:, :, 9 * kz + 3 * ky + kx].reshape(256, 256)
                    term = jnp.dot(rows, weights, preferred_element_type=F32)
                    total = term if total is None else total + term
            acc[kx] = total
        low = pltpu.roll(acc[0], 1, 0).reshape(16, 32, 256)
        high = pltpu.roll(acc[2], 511, 0).reshape(16, 32, 256)
        total = acc[1].reshape(16, 32, 256)
        total = total + jnp.where(edge == 0, 0.0, low) + jnp.where(edge == 31, 0.0, high)
        sums[f, h] = total.reshape(4, 128, 256).astype(BF16)
        for plane in range(4):
            mine = jnp.logical_and(y == x, x == plane)
            away = jnp.logical_not(mine)
            move = links.copy(
                sums.at[f, h, plane], sums_in.at[f, h, y], (p, space(x, zh, plane)),
                sum_sems.at[2 * f + h, y],
            )
            links.sent.append((away, move))
            pl.when(away)(move.start)

            @pl.when(mine)
            def _():
                sums_in[f, h, y] = sums[f, h, plane]

    def gather_sums(f, h):
        for k in range(4):
            mine = jnp.logical_and(y == x, y == k)
            desc = pltpu.make_async_remote_copy(
                src_ref=sums.at[f, h, 0], dst_ref=sums_in.at[f, h, k], send_sem=send_sems.at[0],
                recv_sem=sum_sems.at[2 * f + h, k], device_id=sib, device_id_type=MESH,
            )
            pl.when(jnp.logical_not(mine))(desc.wait_recv)
        total = sums_in[f, h, 0].astype(F32) + sums_in[f, h, 1].astype(F32)
        return total + (sums_in[f, h, 2].astype(F32) + sums_in[f, h, 3].astype(F32))

    def send_top(f, h, value):
        skip = first[f, 4 * h : 4 * h + 4].reshape(128, 256).astype(F32)
        top[p, f, h] = (value + skip).astype(BF16)
        block = top.at[p, f, h]
        return links.start(block, block, across), links.start(block, block, sib)

    def relay_top(f, h, cross):
        cross.wait_recv()
        block = top.at[across[0], f, h]
        return links.start(block, block, sib)

    def add_up(f, chunk, fresh):
        rows = top[chunk, f].reshape(256, 256)
        for t in range(4):
            weights = wu[chunk, :, :, t].reshape(256, 256)
            term = jnp.dot(rows, weights, preferred_element_type=F32)
            if fresh:
                up_acc[f, t] = term
            else:
                up_acc[f, t] += term

    def write(f, out):
        for t in range(4):
            for dx in range(2):
                block = up_acc[f, t, :, 128 * dx : 128 * dx + 128].reshape(8, 32, 128)
                spread[t // 2, :, t % 2, pl.ds(dx, 32, stride=2), :] = block
        fine_out[f] = spread[...].astype(BF16)
        move = pltpu.make_async_copy(fine_out.at[f], out, out_sems.at[f])
        move.start()
        return move

    last = 2 * (1 - zl) + 1 - c
    to_column(0)
    gc.wait()
    to_sibling(0)
    to_column(1)
    convolve(0, 0)
    convolve(0, 1)
    gu.forward_b(ORDER[0])
    gu.forward_b(ORDER[1])
    to_sibling(1)
    convolve(1, 0)
    state = []
    for h in range(2):
        value, gain = silu_gain(gather_sums(0, h))
        keep[h] = gain
        state.append(send_top(0, h, value))
    gu.forward_b(ORDER[2])
    gu.forward_b(ORDER[3])
    convolve(1, 1)
    relays = [relay_top(0, h, state[h][0]) for h in range(2)]
    tangent = [send_top(1, 0, keep[0] * gather_sums(1, 0))]
    for g in ORDER:
        gu.wait_b(g)
    add_up(0, p, True)
    tangent.append(send_top(1, 1, keep[1] * gather_sums(1, 1)))
    for h in range(2):
        state[h][1].wait_recv()
    add_up(0, sib[0], False)
    add_up(0, across[0], False)
    for h in range(2):
        relays[h].wait_recv()
    add_up(0, last, False)
    relays = [relay_top(1, 0, tangent[0][0])]
    moves = [write(0, out_s)]
    add_up(1, p, True)
    relays.append(relay_top(1, 1, tangent[1][0]))
    for h in range(2):
        tangent[h][1].wait_recv()
    add_up(1, sib[0], False)
    add_up(1, across[0], False)
    for h in range(2):
        relays[h].wait_recv()
    add_up(1, last, False)
    moves.append(write(1, out_t))
    for move in moves:
        move.wait()
    links.drain()


def local(fine_state, fine_tangent, down_weight, conv_weight, up_weight):
    vmem = pl.BlockSpec(memory_space=pltpu.VMEM)
    whole = pl.BlockSpec(memory_space=pl.ANY)
    fine = (2, 8, 2, 64, 128)
    shape = jax.ShapeDtypeStruct(fine, BF16)
    state, tangent = pl.pallas_call(
        kernel,
        out_shape=(shape, shape),
        in_specs=[whole, whole, vmem, whole, whole],
        out_specs=(whole, whole),
        scratch_shapes=[
            pltpu.VMEM((2,) + fine, BF16),
            pltpu.VMEM(conv_weight.shape, F32),
            pltpu.VMEM(up_weight.shape, F32),
            pltpu.VMEM(fine, F32),
            pltpu.VMEM((2, 8, 2, 256, 128), BF16),
            pltpu.VMEM((8, 16, 256), BF16),
            pltpu.VMEM((4, 2, 4, 8, 16, 256), BF16),
            pltpu.VMEM((2, 4, 27, 32, 256), BF16),
            pltpu.VMEM((4, 2, 4, 4, 32, 256), BF16),
            pltpu.VMEM((2, 2, 256, 256), BF16),
            pltpu.VMEM((2, 2, 256, 256), BF16),
            pltpu.VMEM((2, 8, 32, 256), BF16),
            pltpu.VMEM((2, 8, 32, 256), BF16),
            pltpu.VMEM((4, 2, 8, 32, 256), BF16),
            pltpu.VMEM((2, 6, 10, 32, 256), BF16),
            pltpu.VMEM((3, 512, 256), F32),
            pltpu.VMEM((2, 128, 256), F32),
            pltpu.VMEM((2, 2, 4, 128, 256), BF16),
            pltpu.VMEM((2, 2, 4, 128, 256), BF16),
            pltpu.VMEM((4, 2, 2, 128, 256), BF16),
            pltpu.VMEM((2, 4, 256, 256), F32),
            pltpu.VMEM(fine, F32),
            pltpu.VMEM((2,) + fine, BF16),
            pltpu.SemaphoreType.DMA((LINKS,)),
            pltpu.SemaphoreType.DMA((LINKS,)),
            pltpu.SemaphoreType.DMA((4, 2)),
            pltpu.SemaphoreType.DMA((6, 2)),
            pltpu.SemaphoreType.DMA((4, 4)),
            pltpu.SemaphoreType.DMA((2,)),
            pltpu.SemaphoreType.DMA((4,)),
        ],
        compiler_params=pltpu.CompilerParams(
            collective_id=0, has_side_effects=True, vmem_limit_bytes=56 * 2**20
        ),
    )(fine_state.reshape(fine), fine_tangent.reshape(fine), down_weight, conv_weight, up_weight)
    return state.reshape(fine_state.shape), tangent.reshape(fine_state.shape)


def solution(mesh):
    in_specs = (
        P("space", None, None, "param"),
        P("space", None, None, "param"),
        P(None, "space", "param"),
        P(None, "space", "param"),
        P(None, "space", "param"),
    )
    out_specs = (P("space", None, None, "param"), P("space", None, None, "param"))
    return jax.shard_map(local, mesh=mesh, in_specs=in_specs, out_specs=out_specs, check_vma=False)
```

```python
import jax
import jax.numpy as jnp
from jax import lax
from jax.experimental import pallas as pl
from jax.experimental.pallas import tpu as pltpu
from jax.sharding import PartitionSpec as P

MESH = pl.DeviceIdType.MESH
F32 = jnp.float32
BF16 = jnp.bfloat16


def silu_gain(primal):
    sigma = jax.nn.sigmoid(primal)
    return primal * sigma, sigma * (1.0 + primal * (1.0 - sigma))


class Links:
    def __init__(self, send_sems, recv_sems, count):
        self.send_sems, self.recv_sems, self.count = send_sems, recv_sems, count
        self.used = 0
        self.sent = []

    def copy(self, src, dst, device, slot=None):
        at = self.used
        self.used += 1
        assert self.used <= self.count
        desc = pltpu.make_async_remote_copy(
            src_ref=src,
            dst_ref=dst,
            send_sem=self.send_sems.at[at],
            recv_sem=self.recv_sems.at[at] if slot is None else slot,
            device_id=device,
            device_id_type=MESH,
        )
        return desc

    def start(self, src, dst, device):
        desc = self.copy(src, dst, device)
        desc.start()
        self.sent.append((None, desc))
        return desc

    def drain(self):
        for cond, desc in self.sent:
            if cond is None:
                desc.wait_send()
            else:
                pl.when(cond)(desc.wait_send)


class Ring:
    def __init__(self, links, view, at, to_z, up, down):
        self.links, self.view, self.to_z, self.up, self.down = links, view, to_z, up, down
        self.zh, self.a = at

    def send(self, z, a, to):
        view = self.view(z, a)
        return self.links.start(view, view, to)

    def start_z(self):
        self.z = self.send(self.zh, self.a, self.to_z)

    def start(self):
        self.own = self.send(self.zh, self.a, self.up), self.send(self.zh, self.a, self.down)

    def after_z(self):
        self.z.wait_recv()
        z = 1 - self.zh
        self.other = self.send(z, self.a, self.up), self.send(z, self.a, self.down)

    def forward(self):
        self.own[0].wait_recv()
        first = self.send(self.zh, (self.a + 3) % 4, self.up)
        self.other[1].wait_recv()
        self.far = first, self.send(1 - self.zh, (self.a + 1) % 4, self.down)

    def wait(self):
        for desc in (self.own[1], self.other[0]) + self.far:
            desc.wait_recv()


class Gather:
    def __init__(self, links, view, at, to_z, to_a, up, down):
        self.links, self.view, self.up, self.down = links, view, up, down
        self.to_z, self.to_a = to_z, to_a
        self.zh, self.a, self.b = at
        self.near, self.first, self.second = {}, {}, {}

    def send(self, z, a, b, to):
        view = self.view(z, a, b)
        return self.links.start(view, view, to)

    def start(self):
        self.near[1, 0] = self.send(self.zh, self.a, self.b, self.to_z)
        for da in (1, 3, 2):
            self.near[0, da] = self.send(self.zh, self.a, self.b, self.to_a((self.a + da) % 4))

    def after_z(self):
        self.near[1, 0].wait_recv()
        for da in (1, 3, 2):
            self.near[1, da] = self.send(1 - self.zh, self.a, self.b, self.to_a((self.a + da) % 4))

    def group(self, g):
        return (self.a + 4 - g) % 4

    def start_b(self, g):
        if g:
            self.near[0, g].wait_recv()
            self.near[1, g].wait_recv()
        a = self.group(g)
        self.first[g] = self.send(None, a, self.b, self.up), self.send(None, a, self.b, self.down)

    def forward_b(self, g):
        a = self.group(g)
        up, down = self.first[g]
        up.wait_recv()
        far = self.send(0, a, (self.b + 3) % 4, self.up)
        down.wait_recv()
        self.second[g] = far, self.send(1, a, (self.b + 1) % 4, self.down)

    def wait_b(self, g):
        for desc in self.second[g]:
            desc.wait_recv()


LINKS = 192
SPLIT = 7
ORDER = (0, 1, 3, 2)


def kernel(
    fs, ft, wd32, wc_in, wu_in, out_s, out_t,
    fine_in, wc32, wu32,
    ff, taps, wd_own, wd, wc, wu, part, part_in, first, first_z, mid, apad, acc, keep, sums, sums_in,
    top, up_acc, spread, fine_out, send_sems, recv_sems, mid_sems, plane_sems, sum_sems, out_sems, in_sems,
):
    loads = []
    for at, (src, dst) in enumerate(
        ((wc_in, wc32), (fs, fine_in.at[0]), (ft, fine_in.at[1]), (wu_in, wu32))
    ):
        loads.append(pltpu.make_async_copy(src, dst, in_sems.at[at]))
        loads[-1].start()
    p = lax.axis_index("param")
    s = lax.axis_index("space")
    zl, c = p // 2, p % 2
    y, zh, x = s // 8, (s // 4) % 2, s % 4

    def space(yy, zz, xx):
        return 8 * yy + 4 * zz + xx

    sib = (2 * zl + 1 - c, s)
    across = (2 * (1 - zl) + c, s)
    swap = (2 * (1 - zl) + c, space((y + 2) % 4, zh, x))
    devs = {
        "zh": (p, space(y, 1 - zh, x)),
        "right": (p, space(y, zh, (x + 1) % 4)),
        "left": (p, space(y, zh, (x + 3) % 4)),
        "up": (p, space((y + 1) % 4, zh, x)),
        "down": (p, space((y + 3) % 4, zh, x)),
    }
    partners = [sib, across, swap]
    partners.append(devs["zh"])
    for step in range(1, 4):
        partners.append((p, space(y, zh, (x + step) % 4)))
        partners.append((p, space((y + step) % 4, zh, x)))
    barrier = pltpu.get_barrier_semaphore()
    for device in partners:
        pl.semaphore_signal(barrier, inc=1, device_id=device, device_id_type=MESH)

    placed = (y // 2) == zl
    wd_own[...] = wd32[...].astype(BF16)

    @pl.when(placed)
    def _():
        wd[y, zh, x] = wd_own[...]

    pl.semaphore_wait(barrier, len(partners))
    links = Links(send_sems, recv_sems, LINKS)

    moved = links.copy(wd_own, wd.at[(y + 2) % 4, zh, x], swap)
    links.sent.append((jnp.logical_not(placed), moved))
    pl.when(jnp.logical_not(placed))(moved.start)
    loads[0].wait()
    wc[zh, x] = wc32[...].astype(BF16)

    def pick(z):
        return slice(None) if z is None else z

    gd = (
        Gather(
            links, lambda z, a, b: wd.at[b, pick(z), a, :SPLIT], (zh, x, y),
            devs["zh"], lambda a: (p, space(y, zh, a)), devs["up"], devs["down"],
        ),
        Gather(
            links, lambda z, a, b: wd.at[a, pick(z), b, SPLIT:], (zh, y, x),
            devs["zh"], lambda a: (p, space(a, zh, x)), devs["right"], devs["left"],
        ),
    )
    gc = Ring(links, lambda z, a: wc.at[z, a], (zh, x), devs["zh"], devs["right"], devs["left"])
    gu = Gather(
        links, lambda z, a, b: wu.at[b, pick(z), a], (zh, x, y),
        devs["zh"], lambda a: (p, space(y, zh, a)), devs["up"], devs["down"],
    )
    gc.start()

    for f in range(2):
        loads[1 + f].wait()
        ff[...] = fine_in[f].astype(F32)
        for dz in range(2):
            for dy in range(2):
                for dx in range(2):
                    rows = ff[dz, :, dy, pl.ds(dx, 32, stride=2), :]
                    taps[c, 4 * dz + 2 * dy + dx, f] = rows.reshape(256, 128).astype(BF16)
    fine_copy = links.start(taps.at[c], taps.at[c], sib)
    pl.when(jnp.logical_not(placed))(moved.wait_recv)
    for part_of in gd:
        part_of.start()
    gc.start_z()
    loads[3].wait()
    for t in range(4):
        for dx in range(2):
            wu[y, zh, x, t, :, 128 * dx : 128 * dx + 128] = wu32[2 * t + dx].astype(BF16)
    for part_of in gd:
        part_of.after_z()
    for g in ORDER:
        gd[0].start_b(g)
        gd[1].start_b(g)
    gc.after_z()
    for g in ORDER:
        gd[0].forward_b(g)
        gd[1].forward_b(g)
    gu.start()
    gc.forward()
    fine_copy.wait_recv()
    for g in ORDER:
        gd[0].wait_b(g)
        gd[1].wait_b(g)

    def down(half, f):
        total = None
        for t in range(8):
            rows = jnp.concatenate([taps[0, t, f], taps[1, t, f]], axis=-1)
            weights = wd[pl.ds(2 * half, 2), :, :, t].reshape(256, 256)
            term = jnp.dot(rows, weights, preferred_element_type=F32)
            total = term if total is None else total + term
        return total

    part_copy = []
    for f in range(2):
        for own in range(2):
            other = down(1 - zl, f) if own == 0 else down(zl, f)
            acc[f, 256 * (1 - own) : 256 * (2 - own)] = other
            part[f, own] = other.astype(BF16)
            part_copy.append(links.start(part.at[f, own], part_in.at[f, own], across))
    gu.after_z()
    apad[:, :, pl.ds(0, 1)] = jnp.zeros((2, 6, 1, 32, 256), BF16)
    apad[:, :, pl.ds(9, 1)] = jnp.zeros((2, 6, 1, 32, 256), BF16)
    last_group = jnp.logical_and(x == 3, zh == 1)
    first_group = jnp.logical_and(x == 0, zh == 0)

    @pl.when(first_group)
    def _():
        apad[:, 0, pl.ds(1, 8)] = jnp.zeros((2, 8, 32, 256), BF16)

    @pl.when(last_group)
    def _():
        apad[:, 5, pl.ds(1, 8)] = jnp.zeros((2, 8, 32, 256), BF16)

    def to_row(block, chunk, f):
        move = links.copy(
            block.at[f], mid.at[y, f], (p, space(chunk, zh, x)), mid_sems.at[y, f]
        )
        away = chunk != y
        links.sent.append((away, move))
        pl.when(away)(move.start)

        @pl.when(chunk == y)
        def _():
            mid[y, f] = block[f]

    for f in range(2):
        for k, block in enumerate((first, first_z)):
            part_copy[2 * f + k].wait_recv()
            pre = acc[f, 256 * k : 256 * k + 256] + part_in[f, k].astype(F32)
            if f == 0:
                value, gain = silu_gain(pre)
                acc[2, 256 * k : 256 * k + 256] = gain
            else:
                value = acc[2, 256 * k : 256 * k + 256] * pre
            block[f] = value.astype(BF16).reshape(8, 32, 256)
            to_row(block, across[0] if k else p, f)
    for g in ORDER:
        gu.start_b(g)

    gets = c == y % 2

    def window(slot, f):
        return apad.at[f, slot, pl.ds(1, 8)]

    def to_column(f):
        for step in ORDER:
            source = (y + step) % 4
            block = mid.at[source, f]
            if step:
                arrived = pltpu.make_async_remote_copy(
                    src_ref=block, dst_ref=block, send_sem=send_sems.at[0],
                    recv_sem=mid_sems.at[source, f], device_id=sib, device_id_type=MESH,
                )
                pl.when(gets)(arrived.wait_recv)
            stays = jnp.logical_and(gets, x == source)
            leaves = jnp.logical_and(gets, x != source)
            main = links.copy(
                block, window(x + 1, f), (p, space(y, zh, source)), plane_sems.at[x + 1, f]
            )
            links.sent.append((leaves, main))
            pl.when(leaves)(main.start)

            @pl.when(stays)
            def _():
                apad[f, x + 1, pl.ds(1, 8)] = mid[source, f]

            plane = space(source, zh, x)
            for slot, edge_x, group, end in (
                (0, 3, (plane + 1) // 4, 31), (5, 0, (plane + 31) // 4, 0)
            ):
                sends = jnp.logical_and(gets, jnp.logical_and(x == edge_x, plane != end))
                to = (p, space(y, group % 2, (group // 2) % 4))
                halo = links.copy(block, window(slot, f), to, plane_sems.at[slot, f])
                links.sent.append((sends, halo))
                pl.when(sends)(halo.start)

    def to_sibling(f):
        for slot in (1, 2, 3, 4, 0, 5):
            view = window(slot, f)
            hop = links.copy(view, view, sib, plane_sems.at[slot, f])
            sends = gets
            if slot == 0:
                arrives = jnp.logical_not(first_group)
                sends = jnp.logical_and(gets, arrives)
            elif slot == 5:
                arrives = jnp.logical_not(last_group)
                sends = jnp.logical_and(gets, arrives)
            else:
                arrives = jnp.logical_not(jnp.logical_and(gets, x == slot - 1))
            pl.when(arrives)(hop.wait_recv)
            links.sent.append((sends, hop))
            pl.when(sends)(hop.start)

    edge = lax.broadcasted_iota(jnp.int32, (1, 32, 1), 1)

    def convolve(f, h):
        for kx in range(3):
            total = None
            for kz in range(3):
                for ky in range(3):
                    rows = apad[f, kz : kz + 4, 4 * h + ky : 4 * h + ky + 4].reshape(512, 256)
                    weights = wc[:, :, 9 * kz + 3 * ky + kx].reshape(256, 256)
                    term = jnp.dot(rows, weights, preferred_element_type=F32)
                    total = term if total is None else total + term
            acc[kx] = total
        low = pltpu.roll(acc[0], 1, 0).reshape(16, 32, 256)
        high = pltpu.roll(acc[2], 511, 0).reshape(16, 32, 256)
        total = acc[1].reshape(16, 32, 256)
        total = total + jnp.where(edge == 0, 0.0, low) + jnp.where(edge == 31, 0.0, high)
        sums[f, h] = total.reshape(4, 128, 256).astype(BF16)
        for plane in range(4):
            mine = jnp.logical_and(y == x, x == plane)
            away = jnp.logical_not(mine)
            move = links.copy(
                sums.at[f, h, plane], sums_in.at[f, h, y], (p, space(x, zh, plane)),
                sum_sems.at[2 * f + h, y],
            )
            links.sent.append((away, move))
            pl.when(away)(move.start)

            @pl.when(mine)
            def _():
                sums_in[f, h, y] = sums[f, h, plane]

    def gather_sums(f, h):
        for k in range(4):
            mine = jnp.logical_and(y == x, y == k)
            desc = pltpu.make_async_remote_copy(
                src_ref=sums.at[f, h, 0], dst_ref=sums_in.at[f, h, k], send_sem=send_sems.at[0],
                recv_sem=sum_sems.at[2 * f + h, k], device_id=sib, device_id_type=MESH,
            )
            pl.when(jnp.logical_not(mine))(desc.wait_recv)
        total = sums_in[f, h, 0].astype(F32) + sums_in[f, h, 1].astype(F32)
        return total + (sums_in[f, h, 2].astype(F32) + sums_in[f, h, 3].astype(F32))

    def send_top(f, h, value):
        skip = first[f, 4 * h : 4 * h + 4].reshape(128, 256).astype(F32)
        top[p, f, h] = (value + skip).astype(BF16)
        block = top.at[p, f, h]
        return links.start(block, block, across), links.start(block, block, sib)

    def relay_top(f, h, cross):
        cross.wait_recv()
        block = top.at[across[0], f, h]
        return links.start(block, block, sib)

    def add_up(f, chunk, fresh):
        rows = top[chunk, f].reshape(256, 256)
        for t in range(4):
            weights = wu[chunk, :, :, t].reshape(256, 256)
            term = jnp.dot(rows, weights, preferred_element_type=F32)
            if fresh:
                up_acc[f, t] = term
            else:
                up_acc[f, t] += term

    def write(f, out):
        for t in range(4):
            for dx in range(2):
                block = up_acc[f, t, :, 128 * dx : 128 * dx + 128].reshape(8, 32, 128)
                spread[t // 2, :, t % 2, pl.ds(dx, 32, stride=2), :] = block
        fine_out[f] = spread[...].astype(BF16)
        move = pltpu.make_async_copy(fine_out.at[f], out, out_sems.at[f])
        move.start()
        return move

    last = 2 * (1 - zl) + 1 - c
    to_column(0)
    to_column(1)
    to_sibling(0)
    gc.wait()
    convolve(0, 0)
    convolve(0, 1)
    gu.forward_b(ORDER[0])
    gu.forward_b(ORDER[1])
    to_sibling(1)
    convolve(1, 0)
    state = []
    for h in range(2):
        value, gain = silu_gain(gather_sums(0, h))
        keep[h] = gain
        state.append(send_top(0, h, value))
    gu.forward_b(ORDER[2])
    gu.forward_b(ORDER[3])
    convolve(1, 1)
    relays = [relay_top(0, h, state[h][0]) for h in range(2)]
    tangent = [send_top(1, 0, keep[0] * gather_sums(1, 0))]
    for g in ORDER:
        gu.wait_b(g)
    add_up(0, p, True)
    tangent.append(send_top(1, 1, keep[1] * gather_sums(1, 1)))
    for h in range(2):
        state[h][1].wait_recv()
    add_up(0, sib[0], False)
    add_up(0, across[0], False)
    for h in range(2):
        relays[h].wait_recv()
    add_up(0, last, False)
    relays = [relay_top(1, 0, tangent[0][0])]
    moves = [write(0, out_s)]
    add_up(1, p, True)
    relays.append(relay_top(1, 1, tangent[1][0]))
    for h in range(2):
        tangent[h][1].wait_recv()
    add_up(1, sib[0], False)
    add_up(1, across[0], False)
    for h in range(2):
        relays[h].wait_recv()
    add_up(1, last, False)
    moves.append(write(1, out_t))
    for move in moves:
        move.wait()
    links.drain()


def local(fine_state, fine_tangent, down_weight, conv_weight, up_weight):
    vmem = pl.BlockSpec(memory_space=pltpu.VMEM)
    whole = pl.BlockSpec(memory_space=pl.ANY)
    fine = (2, 8, 2, 64, 128)
    shape = jax.ShapeDtypeStruct(fine, BF16)
    state, tangent = pl.pallas_call(
        kernel,
        out_shape=(shape, shape),
        in_specs=[whole, whole, vmem, whole, whole],
        out_specs=(whole, whole),
        scratch_shapes=[
            pltpu.VMEM((2,) + fine, BF16),
            pltpu.VMEM(conv_weight.shape, F32),
            pltpu.VMEM(up_weight.shape, F32),
            pltpu.VMEM(fine, F32),
            pltpu.VMEM((2, 8, 2, 256, 128), BF16),
            pltpu.VMEM((8, 16, 256), BF16),
            pltpu.VMEM((4, 2, 4, 8, 16, 256), BF16),
            pltpu.VMEM((2, 4, 27, 32, 256), BF16),
            pltpu.VMEM((4, 2, 4, 4, 32, 256), BF16),
            pltpu.VMEM((2, 2, 256, 256), BF16),
            pltpu.VMEM((2, 2, 256, 256), BF16),
            pltpu.VMEM((2, 8, 32, 256), BF16),
            pltpu.VMEM((2, 8, 32, 256), BF16),
            pltpu.VMEM((4, 2, 8, 32, 256), BF16),
            pltpu.VMEM((2, 6, 10, 32, 256), BF16),
            pltpu.VMEM((3, 512, 256), F32),
            pltpu.VMEM((2, 128, 256), F32),
            pltpu.VMEM((2, 2, 4, 128, 256), BF16),
            pltpu.VMEM((2, 2, 4, 128, 256), BF16),
            pltpu.VMEM((4, 2, 2, 128, 256), BF16),
            pltpu.VMEM((2, 4, 256, 256), F32),
            pltpu.VMEM(fine, F32),
            pltpu.VMEM((2,) + fine, BF16),
            pltpu.SemaphoreType.DMA((LINKS,)),
            pltpu.SemaphoreType.DMA((LINKS,)),
            pltpu.SemaphoreType.DMA((4, 2)),
            pltpu.SemaphoreType.DMA((6, 2)),
            pltpu.SemaphoreType.DMA((4, 4)),
            pltpu.SemaphoreType.DMA((2,)),
            pltpu.SemaphoreType.DMA((4,)),
        ],
        compiler_params=pltpu.CompilerParams(
            collective_id=0, has_side_effects=True, vmem_limit_bytes=56 * 2**20
        ),
    )(fine_state.reshape(fine), fine_tangent.reshape(fine), down_weight, conv_weight, up_weight)
    return state.reshape(fine_state.shape), tangent.reshape(fine_state.shape)


def solution(mesh):
    in_specs = (
        P("space", None, None, "param"),
        P("space", None, None, "param"),
        P(None, "space", "param"),
        P(None, "space", "param"),
        P(None, "space", "param"),
    )
    out_specs = (P("space", None, None, "param"), P("space", None, None, "param"))
    return jax.shard_map(local, mesh=mesh, in_specs=in_specs, out_specs=out_specs, check_vma=False)
```

```python
import jax
import jax.numpy as jnp
from jax import lax
from jax.experimental import pallas as pl
from jax.experimental.pallas import tpu as pltpu
from jax.sharding import PartitionSpec as P

MESH = pl.DeviceIdType.MESH
F32 = jnp.float32
BF16 = jnp.bfloat16


def silu_gain(primal):
    sigma = jax.nn.sigmoid(primal)
    return primal * sigma, sigma * (1.0 + primal * (1.0 - sigma))


class Links:
    def __init__(self, send_sems, recv_sems, count):
        self.send_sems, self.recv_sems, self.count = send_sems, recv_sems, count
        self.used = 0
        self.sent = []

    def copy(self, src, dst, device, slot=None):
        at = self.used
        self.used += 1
        assert self.used <= self.count
        desc = pltpu.make_async_remote_copy(
            src_ref=src,
            dst_ref=dst,
            send_sem=self.send_sems.at[at],
            recv_sem=self.recv_sems.at[at] if slot is None else slot,
            device_id=device,
            device_id_type=MESH,
        )
        return desc

    def start(self, src, dst, device):
        desc = self.copy(src, dst, device)
        desc.start()
        self.sent.append((None, desc))
        return desc

    def drain(self):
        for cond, desc in self.sent:
            if cond is None:
                desc.wait_send()
            else:
                pl.when(cond)(desc.wait_send)


class Ring:
    def __init__(self, links, view, at, to_z, up, down):
        self.links, self.view, self.to_z, self.up, self.down = links, view, to_z, up, down
        self.zh, self.a = at

    def send(self, z, a, to):
        view = self.view(z, a)
        return self.links.start(view, view, to)

    def start_z(self):
        self.z = self.send(self.zh, self.a, self.to_z)

    def start(self):
        self.own = self.send(self.zh, self.a, self.up), self.send(self.zh, self.a, self.down)

    def after_z(self):
        self.z.wait_recv()
        z = 1 - self.zh
        self.other = self.send(z, self.a, self.up), self.send(z, self.a, self.down)

    def forward(self):
        self.own[0].wait_recv()
        first = self.send(self.zh, (self.a + 3) % 4, self.up)
        self.other[1].wait_recv()
        self.far = first, self.send(1 - self.zh, (self.a + 1) % 4, self.down)

    def wait(self):
        for desc in (self.own[1], self.other[0]) + self.far:
            desc.wait_recv()


class Gather:
    def __init__(self, links, view, at, to_z, to_a, up, down):
        self.links, self.view, self.up, self.down = links, view, up, down
        self.to_z, self.to_a = to_z, to_a
        self.zh, self.a, self.b = at
        self.near, self.first, self.second = {}, {}, {}

    def send(self, z, a, b, to):
        view = self.view(z, a, b)
        return self.links.start(view, view, to)

    def start(self):
        self.near[1, 0] = self.send(self.zh, self.a, self.b, self.to_z)
        for da in (1, 3, 2):
            self.near[0, da] = self.send(self.zh, self.a, self.b, self.to_a((self.a + da) % 4))

    def after_z(self):
        self.near[1, 0].wait_recv()
        for da in (1, 3, 2):
            self.near[1, da] = self.send(1 - self.zh, self.a, self.b, self.to_a((self.a + da) % 4))

    def group(self, g):
        return (self.a + 4 - g) % 4

    def start_b(self, g):
        if g:
            self.near[0, g].wait_recv()
            self.near[1, g].wait_recv()
        a = self.group(g)
        self.first[g] = self.send(None, a, self.b, self.up), self.send(None, a, self.b, self.down)

    def forward_b(self, g):
        a = self.group(g)
        up, down = self.first[g]
        up.wait_recv()
        far = self.send(0, a, (self.b + 3) % 4, self.up)
        down.wait_recv()
        self.second[g] = far, self.send(1, a, (self.b + 1) % 4, self.down)

    def wait_b(self, g):
        for desc in self.second[g]:
            desc.wait_recv()


LINKS = 192
SPLIT = 7
ORDER = (0, 1, 3, 2)


def kernel(
    fs, ft, wd32, wc_in, wu_in, out_s, out_t,
    fine_in, wc32, wu32,
    ff, taps, wd_own, wd, wc, wu, part, part_in, first, first_z, mid, apad, acc, keep, sums, sums_in,
    top, up_acc, spread, fine_out, send_sems, recv_sems, mid_sems, plane_sems, sum_sems, out_sems, in_sems,
):
    loads = []
    for at, (src, dst) in enumerate(
        ((wc_in, wc32), (fs, fine_in.at[0]), (ft, fine_in.at[1]), (wu_in, wu32))
    ):
        loads.append(pltpu.make_async_copy(src, dst, in_sems.at[at]))
        loads[-1].start()
    p = lax.axis_index("param")
    s = lax.axis_index("space")
    zl, c = p // 2, p % 2
    y, zh, x = s // 8, (s // 4) % 2, s % 4

    def space(yy, zz, xx):
        return 8 * yy + 4 * zz + xx

    sib = (2 * zl + 1 - c, s)
    across = (2 * (1 - zl) + c, s)
    swap = (2 * (1 - zl) + c, space((y + 2) % 4, zh, x))
    devs = {
        "zh": (p, space(y, 1 - zh, x)),
        "right": (p, space(y, zh, (x + 1) % 4)),
        "left": (p, space(y, zh, (x + 3) % 4)),
        "up": (p, space((y + 1) % 4, zh, x)),
        "down": (p, space((y + 3) % 4, zh, x)),
    }
    partners = [sib, across, swap]
    partners.append(devs["zh"])
    for step in range(1, 4):
        partners.append((p, space(y, zh, (x + step) % 4)))
        partners.append((p, space((y + step) % 4, zh, x)))
    barrier = pltpu.get_barrier_semaphore()
    for device in partners:
        pl.semaphore_signal(barrier, inc=1, device_id=device, device_id_type=MESH)

    placed = (y // 2) == zl
    wd_own[...] = wd32[...].astype(BF16)

    @pl.when(placed)
    def _():
        wd[y, zh, x] = wd_own[...]

    pl.semaphore_wait(barrier, len(partners))
    links = Links(send_sems, recv_sems, LINKS)

    moved = links.copy(wd_own, wd.at[(y + 2) % 4, zh, x], swap)
    links.sent.append((jnp.logical_not(placed), moved))
    pl.when(jnp.logical_not(placed))(moved.start)
    loads[0].wait()
    wc[zh, x] = wc32[...].astype(BF16)

    def pick(z):
        return slice(None) if z is None else z

    gd = (
        Gather(
            links, lambda z, a, b: wd.at[b, pick(z), a, :SPLIT], (zh, x, y),
            devs["zh"], lambda a: (p, space(y, zh, a)), devs["up"], devs["down"],
        ),
        Gather(
            links, lambda z, a, b: wd.at[a, pick(z), b, SPLIT:], (zh, y, x),
            devs["zh"], lambda a: (p, space(a, zh, x)), devs["right"], devs["left"],
        ),
    )
    gc = Ring(links, lambda z, a: wc.at[z, a], (zh, x), devs["zh"], devs["right"], devs["left"])
    gu = Gather(
        links, lambda z, a, b: wu.at[b, pick(z), a], (zh, x, y),
        devs["zh"], lambda a: (p, space(y, zh, a)), devs["up"], devs["down"],
    )
    gc.start()

    for f in range(2):
        loads[1 + f].wait()
        ff[...] = fine_in[f].astype(F32)
        for dz in range(2):
            for dy in range(2):
                for dx in range(2):
                    rows = ff[dz, :, dy, pl.ds(dx, 32, stride=2), :]
                    taps[c, 4 * dz + 2 * dy + dx, f] = rows.reshape(256, 128).astype(BF16)
    fine_copy = links.start(taps.at[c], taps.at[c], sib)
    pl.when(jnp.logical_not(placed))(moved.wait_recv)
    for part_of in gd:
        part_of.start()
    gc.start_z()
    loads[3].wait()
    for t in range(4):
        for dx in range(2):
            wu[y, zh, x, t, :, 128 * dx : 128 * dx + 128] = wu32[2 * t + dx].astype(BF16)
    for part_of in gd:
        part_of.after_z()
    for g in ORDER:
        gd[0].start_b(g)
        gd[1].start_b(g)
    gc.after_z()
    for g in ORDER:
        gd[0].forward_b(g)
        gd[1].forward_b(g)
    gu.start()
    gc.forward()
    fine_copy.wait_recv()
    for g in ORDER:
        gd[0].wait_b(g)
        gd[1].wait_b(g)

    def down(half, f):
        total = None
        for t in range(8):
            rows = jnp.concatenate([taps[0, t, f], taps[1, t, f]], axis=-1)
            weights = wd[pl.ds(2 * half, 2), :, :, t].reshape(256, 256)
            term = jnp.dot(rows, weights, preferred_element_type=F32)
            total = term if total is None else total + term
        return total

    part_copy = []
    for f in range(2):
        for own in range(2):
            other = down(1 - zl, f) if own == 0 else down(zl, f)
            acc[f, 256 * (1 - own) : 256 * (2 - own)] = other
            part[f, own] = other.astype(BF16)
            part_copy.append(links.start(part.at[f, own], part_in.at[f, own], across))
    gu.after_z()
    apad[:, :, pl.ds(0, 1)] = jnp.zeros((2, 6, 1, 32, 256), BF16)
    apad[:, :, pl.ds(9, 1)] = jnp.zeros((2, 6, 1, 32, 256), BF16)
    last_group = jnp.logical_and(x == 3, zh == 1)
    first_group = jnp.logical_and(x == 0, zh == 0)

    @pl.when(first_group)
    def _():
        apad[:, 0, pl.ds(1, 8)] = jnp.zeros((2, 8, 32, 256), BF16)

    @pl.when(last_group)
    def _():
        apad[:, 5, pl.ds(1, 8)] = jnp.zeros((2, 8, 32, 256), BF16)

    def to_row(block, chunk, f):
        move = links.copy(
            block.at[f], mid.at[y, f], (p, space(chunk, zh, x)), mid_sems.at[y, f]
        )
        away = chunk != y
        links.sent.append((away, move))
        pl.when(away)(move.start)

        @pl.when(chunk == y)
        def _():
            mid[y, f] = block[f]

    for f in range(2):
        for k, block in enumerate((first, first_z)):
            part_copy[2 * f + k].wait_recv()
            pre = acc[f, 256 * k : 256 * k + 256] + part_in[f, k].astype(F32)
            if f == 0:
                value, gain = silu_gain(pre)
                acc[2, 256 * k : 256 * k + 256] = gain
            else:
                value = acc[2, 256 * k : 256 * k + 256] * pre
            block[f] = value.astype(BF16).reshape(8, 32, 256)
            to_row(block, across[0] if k else p, f)
    for g in ORDER:
        gu.start_b(g)

    gets = c == y % 2

    def window(slot, f):
        return apad.at[f, slot, pl.ds(1, 8)]

    def to_column(f):
        for step in ORDER:
            source = (y + step) % 4
            block = mid.at[source, f]
            if step:
                arrived = pltpu.make_async_remote_copy(
                    src_ref=block, dst_ref=block, send_sem=send_sems.at[0],
                    recv_sem=mid_sems.at[source, f], device_id=sib, device_id_type=MESH,
                )
                pl.when(gets)(arrived.wait_recv)
            stays = jnp.logical_and(gets, x == source)
            leaves = jnp.logical_and(gets, x != source)
            main = links.copy(
                block, window(x + 1, f), (p, space(y, zh, source)), plane_sems.at[x + 1, f]
            )
            links.sent.append((leaves, main))
            pl.when(leaves)(main.start)

            @pl.when(stays)
            def _():
                apad[f, x + 1, pl.ds(1, 8)] = mid[source, f]

            plane = space(source, zh, x)
            for slot, edge_x, group, end in (
                (0, 3, (plane + 1) // 4, 31), (5, 0, (plane + 31) // 4, 0)
            ):
                sends = jnp.logical_and(gets, jnp.logical_and(x == edge_x, plane != end))
                to = (p, space(y, group % 2, (group // 2) % 4))
                halo = links.copy(block, window(slot, f), to, plane_sems.at[slot, f])
                links.sent.append((sends, halo))
                pl.when(sends)(halo.start)

    def to_sibling(f):
        for slot in (1, 2, 3, 4, 0, 5):
            view = window(slot, f)
            hop = links.copy(view, view, sib, plane_sems.at[slot, f])
            sends = gets
            if slot == 0:
                arrives = jnp.logical_not(first_group)
                sends = jnp.logical_and(gets, arrives)
            elif slot == 5:
                arrives = jnp.logical_not(last_group)
                sends = jnp.logical_and(gets, arrives)
            else:
                arrives = jnp.logical_not(jnp.logical_and(gets, x == slot - 1))
            pl.when(arrives)(hop.wait_recv)
            links.sent.append((sends, hop))
            pl.when(sends)(hop.start)

    edge = lax.broadcasted_iota(jnp.int32, (1, 32, 1), 1)

    def convolve(f, h):
        for kx in range(3):
            total = None
            for kz in range(3):
                for ky in range(3):
                    rows = apad[f, kz : kz + 4, 4 * h + ky : 4 * h + ky + 4].reshape(512, 256)
                    weights = wc[:, :, 9 * kz + 3 * ky + kx].reshape(256, 256)
                    term = jnp.dot(rows, weights, preferred_element_type=F32)
                    total = term if total is None else total + term
            acc[kx] = total
        low = pltpu.roll(acc[0], 1, 0).reshape(16, 32, 256)
        high = pltpu.roll(acc[2], 511, 0).reshape(16, 32, 256)
        total = acc[1].reshape(16, 32, 256)
        total = total + jnp.where(edge == 0, 0.0, low) + jnp.where(edge == 31, 0.0, high)
        sums[f, h] = total.reshape(4, 128, 256).astype(BF16)
        for plane in range(4):
            mine = jnp.logical_and(y == x, x == plane)
            away = jnp.logical_not(mine)
            move = links.copy(
                sums.at[f, h, plane], sums_in.at[f, h, y], (p, space(x, zh, plane)),
                sum_sems.at[2 * f + h, y],
            )
            links.sent.append((away, move))
            pl.when(away)(move.start)

            @pl.when(mine)
            def _():
                sums_in[f, h, y] = sums[f, h, plane]

    def gather_sums(f, h):
        for k in range(4):
            mine = jnp.logical_and(y == x, y == k)
            desc = pltpu.make_async_remote_copy(
                src_ref=sums.at[f, h, 0], dst_ref=sums_in.at[f, h, k], send_sem=send_sems.at[0],
                recv_sem=sum_sems.at[2 * f + h, k], device_id=sib, device_id_type=MESH,
            )
            pl.when(jnp.logical_not(mine))(desc.wait_recv)
        total = sums_in[f, h, 0].astype(F32) + sums_in[f, h, 1].astype(F32)
        return total + (sums_in[f, h, 2].astype(F32) + sums_in[f, h, 3].astype(F32))

    def send_top(f, h, value):
        skip = first[f, 4 * h : 4 * h + 4].reshape(128, 256).astype(F32)
        top[p, f, h] = (value + skip).astype(BF16)
        block = top.at[p, f, h]
        return links.start(block, block, across), links.start(block, block, sib)

    def relay_top(f, h, cross):
        cross.wait_recv()
        block = top.at[across[0], f, h]
        return links.start(block, block, sib)

    def add_up(f, chunk, fresh):
        rows = top[chunk, f].reshape(256, 256)
        for t in range(4):
            weights = wu[chunk, :, :, t].reshape(256, 256)
            term = jnp.dot(rows, weights, preferred_element_type=F32)
            if fresh:
                up_acc[f, t] = term
            else:
                up_acc[f, t] += term

    def write(f, out):
        for t in range(4):
            for dx in range(2):
                block = up_acc[f, t, :, 128 * dx : 128 * dx + 128].reshape(8, 32, 128)
                spread[t // 2, :, t % 2, pl.ds(dx, 32, stride=2), :] = block
        fine_out[f] = spread[...].astype(BF16)
        move = pltpu.make_async_copy(fine_out.at[f], out, out_sems.at[f])
        move.start()
        return move

    last = 2 * (1 - zl) + 1 - c
    to_column(0)
    to_column(1)
    to_sibling(0)
    gc.wait()
    convolve(0, 0)
    convolve(0, 1)
    gu.forward_b(ORDER[0])
    gu.forward_b(ORDER[1])
    to_sibling(1)
    convolve(1, 0)
    state = []
    for h in range(2):
        value, gain = silu_gain(gather_sums(0, h))
        keep[h] = gain
        state.append(send_top(0, h, value))
    gu.forward_b(ORDER[2])
    gu.forward_b(ORDER[3])
    convolve(1, 1)
    relays = [relay_top(0, h, state[h][0]) for h in range(2)]
    tangent = [send_top(1, 0, keep[0] * gather_sums(1, 0))]
    for g in ORDER:
        gu.wait_b(g)
    add_up(0, p, True)
    tangent.append(send_top(1, 1, keep[1] * gather_sums(1, 1)))
    for h in range(2):
        state[h][1].wait_recv()
    add_up(0, sib[0], False)
    add_up(0, across[0], False)
    ahead = relay_top(1, 0, tangent[0][0])
    for h in range(2):
        relays[h].wait_recv()
    add_up(0, last, False)
    relays = [ahead]
    moves = [write(0, out_s)]
    add_up(1, p, True)
    relays.append(relay_top(1, 1, tangent[1][0]))
    for h in range(2):
        tangent[h][1].wait_recv()
    add_up(1, sib[0], False)
    add_up(1, across[0], False)
    for h in range(2):
        relays[h].wait_recv()
    add_up(1, last, False)
    moves.append(write(1, out_t))
    for move in moves:
        move.wait()
    links.drain()


def local(fine_state, fine_tangent, down_weight, conv_weight, up_weight):
    vmem = pl.BlockSpec(memory_space=pltpu.VMEM)
    whole = pl.BlockSpec(memory_space=pl.ANY)
    fine = (2, 8, 2, 64, 128)
    shape = jax.ShapeDtypeStruct(fine, BF16)
    state, tangent = pl.pallas_call(
        kernel,
        out_shape=(shape, shape),
        in_specs=[whole, whole, vmem, whole, whole],
        out_specs=(whole, whole),
        scratch_shapes=[
            pltpu.VMEM((2,) + fine, BF16),
            pltpu.VMEM(conv_weight.shape, F32),
            pltpu.VMEM(up_weight.shape, F32),
            pltpu.VMEM(fine, F32),
            pltpu.VMEM((2, 8, 2, 256, 128), BF16),
            pltpu.VMEM((8, 16, 256), BF16),
            pltpu.VMEM((4, 2, 4, 8, 16, 256), BF16),
            pltpu.VMEM((2, 4, 27, 32, 256), BF16),
            pltpu.VMEM((4, 2, 4, 4, 32, 256), BF16),
            pltpu.VMEM((2, 2, 256, 256), BF16),
            pltpu.VMEM((2, 2, 256, 256), BF16),
            pltpu.VMEM((2, 8, 32, 256), BF16),
            pltpu.VMEM((2, 8, 32, 256), BF16),
            pltpu.VMEM((4, 2, 8, 32, 256), BF16),
            pltpu.VMEM((2, 6, 10, 32, 256), BF16),
            pltpu.VMEM((3, 512, 256), F32),
            pltpu.VMEM((2, 128, 256), F32),
            pltpu.VMEM((2, 2, 4, 128, 256), BF16),
            pltpu.VMEM((2, 2, 4, 128, 256), BF16),
            pltpu.VMEM((4, 2, 2, 128, 256), BF16),
            pltpu.VMEM((2, 4, 256, 256), F32),
            pltpu.VMEM(fine, F32),
            pltpu.VMEM((2,) + fine, BF16),
            pltpu.SemaphoreType.DMA((LINKS,)),
            pltpu.SemaphoreType.DMA((LINKS,)),
            pltpu.SemaphoreType.DMA((4, 2)),
            pltpu.SemaphoreType.DMA((6, 2)),
            pltpu.SemaphoreType.DMA((4, 4)),
            pltpu.SemaphoreType.DMA((2,)),
            pltpu.SemaphoreType.DMA((4,)),
        ],
        compiler_params=pltpu.CompilerParams(
            collective_id=0, has_side_effects=True, vmem_limit_bytes=56 * 2**20
        ),
    )(fine_state.reshape(fine), fine_tangent.reshape(fine), down_weight, conv_weight, up_weight)
    return state.reshape(fine_state.shape), tangent.reshape(fine_state.shape)


def solution(mesh):
    in_specs = (
        P("space", None, None, "param"),
        P("space", None, None, "param"),
        P(None, "space", "param"),
        P(None, "space", "param"),
        P(None, "space", "param"),
    )
    out_specs = (P("space", None, None, "param"), P("space", None, None, "param"))
    return jax.shard_map(local, mesh=mesh, in_specs=in_specs, out_specs=out_specs, check_vma=False)
```
